32 devices in a mesh: var: 8 (over y, x, core), smp: 4 (over z).
Axes of the slice: x: 2, y: 2, z: 4, core: 2. Of those that a mesh axis runs over, the one named last changes fastest.
Arguments:
- dosage: bfloat16 [4096, 4096], P('smp', 'var'), may hold values from -6 to 6
- trait_class: int32 [4096], P('smp'), may hold values from 0 to 15
- class_effect: float32 [16], replicated, may hold values from -4 to 4
Outputs:
- interaction: float32 [4096, 1536], P(('var', 'smp'))
The draws below stay inside these ranges and needn't reach their ends.
All inputs are finite; a program needn't handle non-finite values.
Results may differ from the reference program's by a relative error of at most 0.0029.
Values may be sent and summed in bfloat16 or wider, within the bound.
A program may use at most 64 MiB of HBM per device.

```python
import jax
import jax.numpy as jnp
from jax import lax

VAR_DEV = 512
CLASSES = 16
SAMPLES = 4096
VARIANTS = 4096
N_VAR = 8


def set_ends(drawn, key, least, high):
    longest = drawn.shape.index(max(drawn.shape))
    spots = []
    for shift in (0, 1):
        where = [jax.random.randint(jax.random.fold_in(key, axis), (), 0, length) for axis, length in enumerate(drawn.shape)]
        where[longest] = (where[longest] + shift) % drawn.shape[longest]
        spots.append(tuple(where))
    return drawn.at[spots[0]].set(least).at[spots[1]].set(high)


def steps_of(key, shape, cuts, least, largest):
    def one(dim, blocks):
        draws = jax.random.uniform(jax.random.fold_in(jax.random.fold_in(key, 6), dim), (blocks,), jnp.float32, least / len(cuts), largest / len(cuts))
        return jnp.repeat(jnp.exp(draws), shape[dim] // blocks).reshape((-1,) + (1,) * (len(shape) - dim - 1))

    factor_of = one(*cuts[0])
    for cut in cuts[1:]:
        factor_of = factor_of * one(*cut)
    return factor_of


def bell_draw(rng, dims, scale, most, cuts=(), kind=jnp.bfloat16):
    gain = steps_of(rng, dims, cuts, -0.22, 0.18) if cuts else 1.0
    drawn = jax.random.normal(rng, dims, jnp.float32) * scale * gain
    return jnp.minimum(jnp.maximum(drawn, -most), most).astype(kind)


def setup_inputs(seed: int = 0) -> dict:
    seeds = jax.random.split(jax.random.key(seed), 4)
    return {
        "dosage": bell_draw(seeds[0], (SAMPLES, VARIANTS), 1.0, 6.0, ((0, 4), (1, 8))),
        "trait_class": set_ends(jax.random.randint(seeds[1], (SAMPLES,), 0, CLASSES), jax.random.fold_in(seeds[1], 1), 0, CLASSES - 1).astype(jnp.int32),
        "class_effect": bell_draw(seeds[2], (CLASSES,), 1.0, 4.0, (), jnp.float32),
    }


def reference(dosage, trait_class, class_effect):
    centred = class_effect - jnp.mean(class_effect)
    picks = trait_class[:, None] == jnp.arange(CLASSES, dtype=jnp.int32)[None, :]
    trait = lax.optimization_barrier(jnp.sum(jnp.where(picks, centred[None, :], jnp.float32(0.0)), axis=1))

    def one_block(block):

        def take(index):
            start = (jnp.mod(index, N_VAR) * VAR_DEV).astype(jnp.int32)
            return lax.dynamic_slice_in_dim(dosage, start, VAR_DEV, 1)
        own = take(block)
        right = jnp.concatenate([take(block - 1), own, take(block + 1)], axis=1)
        own_values = own.astype(jnp.float32)
        weighted = (trait[:, None] * own_values).astype(jnp.bfloat16)
        squared = (own_values * own_values).astype(jnp.bfloat16)
        right_values = right.astype(jnp.float32)
        right_sq = (right_values * right_values).astype(jnp.bfloat16)
        cross = jnp.dot(weighted.T, right, preferred_element_type=jnp.float32)
        fourth = jnp.dot(squared.T, right_sq, preferred_element_type=jnp.float32)
        return cross / jnp.sqrt(fourth + 1e-05)
    blocks = lax.map(one_block, jnp.arange(N_VAR, dtype=jnp.int32))
    return blocks.reshape(VARIANTS, 3 * VAR_DEV)
```

```python
import functools

import jax
import jax.numpy as jnp
from jax import lax
from jax.experimental import pallas as pl
from jax.experimental.pallas import tpu as pltpu
from jax.sharding import PartitionSpec as P

MESH = pl.DeviceIdType.MESH
F32, BF16 = jnp.float32, jnp.bfloat16
LANES = 128
EXTRA = 16


def kernel(
    nv, n, dosage_ref, class_hbm, effect_hbm, out_ref,
    d_ref, class_ref, effect_ref, after, wt, qt, sq, turned, before, own_turned, mirrored,
    own_part, own_wire, own_relay, own_fwd, own_summed, own_direct,
    next_part, next_wire, next_relay, next_fwd, next_summed, next_direct,
    load_sem, d_send, d_recv, t_send, t_recv, m_send, m_recv,
    own_rs, own_rr, own_fs, own_sr, own_ds, own_dr,
    next_rs, next_rr, next_fs, next_sr, next_ds, next_dr,
):
    depth, width = d_ref.shape
    rows, half, pairs = width // n, width // 2, n // 2
    fold = rows % LANES == 0
    v, s = lax.axis_index("var"), lax.axis_index("smp")
    nxt, prv = lax.rem(v + 1, nv), lax.rem(v + nv - 1, nv)
    pair, odd = s // 2, lax.rem(s, 2)
    partner = s + 1 - 2 * odd

    loads = [
        pltpu.make_async_copy(dosage_ref, d_ref, load_sem.at[0]),
        pltpu.make_async_copy(class_hbm, class_ref, load_sem.at[1]),
        pltpu.make_async_copy(effect_hbm, effect_ref, load_sem.at[2]),
    ]
    for load in loads:
        load.start()
    barrier = pltpu.get_barrier_semaphore()
    for near in (nxt, prv):
        for step in range(n):
            pl.semaphore_signal(barrier, inc=1, device_id=(near, lax.rem(s + step, n)), device_id_type=MESH)
    for step in range(1, n):
        pl.semaphore_signal(barrier, inc=1, device_id=(v, lax.rem(s + step, n)), device_id_type=MESH)
    for load in loads:
        load.wait()

    def cols(h):
        return slice(h * half, (h + 1) * half)

    def shift(h):
        return pltpu.make_async_remote_copy(
            src_ref=d_ref.at[:, cols(h)], dst_ref=after.at[:, cols(h)],
            send_sem=d_send.at[h], recv_sem=d_recv.at[h],
            device_id=(prv, s), device_id_type=MESH,
        )

    classes = effect_ref.shape[0]
    mean = effect_ref[0]
    for c in range(1, classes):
        mean = mean + effect_ref[c]
    mean = mean / classes
    picked = class_ref[...]
    trait = jnp.zeros(picked.shape, F32)
    for c in range(classes):
        trait = jnp.where(picked == c, effect_ref[c] - mean, trait)
    for at in range(0, width, LANES):
        values = d_ref[:, at:at + LANES].astype(F32).T
        wt[at:at + LANES, :] = (values * trait).astype(BF16)
        qt[at:at + LANES, :] = (values * values).astype(BF16)

    def owns(a, c):
        from_a, from_c = abs_of(2 * a - (n - 1)), abs_of(2 * c - (n - 1))
        return jnp.logical_or(from_a > from_c, jnp.logical_and(from_a == from_c, a < c))

    def abs_of(x):
        return lax.max(x, -x) if isinstance(x, jax.Array) else jnp.int32(abs(x))

    def extent(t):
        if not fold:
            return slice(0, width)
        first, last = (t, n - 1 - t) if t < pairs else (n - t, t)
        return slice(first * rows, (last + 1) * rows)

    def cases(index, count, body):
        for known in range(count):
            pl.when(index == known)(functools.partial(body, known))

    def at_rows(index):
        return pl.ds(pl.multiple_of(index * rows, rows), rows)

    def outer(k):
        higher = lax.rem(pair + k, pairs) > pair
        return jnp.logical_or(
            jnp.logical_and(higher, odd == 0), jnp.logical_and(jnp.logical_not(higher), odd == 1)
        )

    class Group:
        def __init__(self, folded, part, wire, relay, fwd, summed, direct, rs, rr, fs, sr, ds, dr):
            self.folded, self.part, self.wire, self.relay = folded, part, wire, relay
            self.fwd, self.summed, self.direct = fwd, summed, direct
            self.rs, self.rr, self.fs, self.sr, self.ds, self.dr = rs, rr, fs, sr, ds, dr

        def span(self, t):
            return extent(t) if self.folded else slice(None)

        def by(self, index, count, body):
            if self.folded:
                cases(index, count, body)
            else:
                body(index)

        def relay_copy(self, u, other, j):
            t = 2 * other + j
            span = self.span(t)
            return pltpu.make_async_remote_copy(
                src_ref=self.wire.at[u, at_rows(t), span], dst_ref=self.relay.at[u, other, j, :, span],
                send_sem=self.rs.at[u, other, j], recv_sem=self.rr.at[u, other, j],
                device_id=(v, partner), device_id_type=MESH,
            )

        def fwd_copy(self, u, other, j):
            t = 2 * other + j
            span = self.span(t)
            return pltpu.make_async_remote_copy(
                src_ref=self.fwd.at[u, other, j, :, span], dst_ref=self.summed.at[u, pair, :, span],
                send_sem=self.fs.at[u, other, j], recv_sem=self.sr.at[u, pair],
                device_id=(v, t), device_id_type=MESH,
            )

        def sum_wait(self, u, source, t):
            span = self.span(t)
            here = self.summed.at[u, source, :, span]
            pltpu.make_async_remote_copy(
                src_ref=here, dst_ref=here, send_sem=self.fs.at[u, source, 0], recv_sem=self.sr.at[u, source],
                device_id=(v, partner), device_id_type=MESH,
            ).wait_recv()

        def dir_copy(self, u, t):
            span = self.span(t)
            return pltpu.make_async_remote_copy(
                src_ref=self.wire.at[u, at_rows(t), span], dst_ref=self.direct.at[u, :, span],
                send_sem=self.ds.at[u], recv_sem=self.dr.at[u],
                device_id=(v, partner), device_id_type=MESH,
            )

        def product(self, u, left, right):
            got = jnp.dot(left[...], right, preferred_element_type=F32)
            self.part[u] = got
            self.wire[u] = got.astype(BF16)

        def send_relays(self, u):
            for k in range(1, pairs):
                @pl.when(outer(k))
                def _():
                    def send(other):
                        for j in range(2):
                            self.relay_copy(u, other, j).start()

                    self.by(lax.rem(pair + k, pairs), pairs, send)

        def send_sums(self, u):
            for k in range(1, pairs):
                @pl.when(jnp.logical_not(outer(k)))
                def _():
                    def send(other):
                        for j in range(2):
                            self.relay_copy(u, other, j).wait_recv()
                            own = self.part[u, at_rows(2 * other + j), :]
                            self.fwd[u, other, j] = (own + self.relay[u, other, j].astype(F32)).astype(BF16)
                            self.fwd_copy(u, other, j).start()

                    self.by(lax.rem(pair + k, pairs), pairs, send)

        def send_direct(self, u):
            self.by(partner, n, lambda t: self.dir_copy(u, t).start())

        def total(self, u):
            def wait(t):
                self.dir_copy(u, t).wait_recv()
                for k in range(1, pairs):
                    self.sum_wait(u, lax.rem(pair + k, pairs), t)

            self.by(s, n, wait)
            got = self.part[u, at_rows(s), :] + self.direct[u].astype(F32)
            for k in range(1, pairs):
                got = got + self.summed[u, lax.rem(pair + k, pairs)].astype(F32)
            return got

        def finish(self, units):
            for u in range(units):
                self.by(partner, n, lambda t: self.dir_copy(u, t).wait_send())
                for k in range(1, pairs):
                    def relays(other):
                        for j in range(2):
                            self.relay_copy(u, other, j).wait_send()

                    def sums(other):
                        for j in range(2):
                            self.fwd_copy(u, other, j).wait_send()

                    other = lax.rem(pair + k, pairs)

                    @pl.when(outer(k))
                    def _():
                        self.by(other, pairs, relays)

                    @pl.when(jnp.logical_not(outer(k)))
                    def _():
                        self.by(other, pairs, sums)

    own = Group(
        fold, own_part, own_wire, own_relay, own_fwd, own_summed, own_direct,
        own_rs, own_rr, own_fs, own_sr, own_ds, own_dr,
    )
    follow = Group(
        False, next_part, next_wire, next_relay, next_fwd, next_summed, next_direct,
        next_rs, next_rr, next_fs, next_sr, next_ds, next_dr,
    )

    def squares(values):
        values = values.astype(F32)
        return (values * values).astype(BF16)

    own.product(0, wt, d_ref[...])
    pl.semaphore_wait(barrier, 3 * n - 1)
    for h in range(2):
        shift(h).start()
    own.send_relays(0)
    sq[...] = squares(d_ref[...])
    own.product(1, qt, sq[...])
    own.send_relays(1)
    late = outer(1) if pairs > 1 else jnp.logical_and(odd == 0, odd == 1)

    for u in range(2):
        own.send_direct(u)
    for h in range(2):
        shift(h).wait_recv()
        follow.product(2 * h, wt, after[:, cols(h)])
        follow.send_relays(2 * h)
        sq[:, cols(h)] = squares(after[:, cols(h)])
        follow.product(2 * h + 1, qt, sq[:, cols(h)])
        follow.send_relays(2 * h + 1)

        @pl.when(jnp.logical_not(late))
        def _():
            for u in range(2 * h, 2 * h + 2):
                follow.send_direct(u)

        if h == 0:
            for u in range(2):
                own.send_sums(u)

    @pl.when(late)
    def _():
        for u in range(4):
            follow.send_direct(u)

    for u in range(4):
        follow.send_sums(u)

    def turn_copy(t, slot):
        return pltpu.make_async_remote_copy(
            src_ref=turned.at[t * rows:(t + 1) * rows], dst_ref=before.at[slot],
            send_sem=t_send.at[t], recv_sem=t_recv.at[slot],
            device_id=(nxt, t), device_id_type=MESH,
        )

    def mirror_copy(t, slot):
        return pltpu.make_async_remote_copy(
            src_ref=own_turned.at[t * rows:(t + 1) * rows], dst_ref=mirrored.at[slot],
            send_sem=m_send.at[t], recv_sem=m_recv.at[slot],
            device_id=(v, t), device_id_type=MESH,
        )

    for h in range(2):
        stat = follow.total(2 * h) / jnp.sqrt(follow.total(2 * h + 1) + 1e-05)
        out_ref[:, 2 * width + h * half:2 * width + (h + 1) * half] = stat
        turned[cols(h), :] = stat.T.astype(BF16)
        for t in range(h * pairs, (h + 1) * pairs):
            turn_copy(t, s).start()
    stat = own.total(0) / jnp.sqrt(own.total(1) + 1e-05)
    if fold:
        own_turned[...] = stat.T.astype(BF16)
        for t in range(n):
            @pl.when(owns(s, t))
            def _():
                mirror_copy(t, s).start()
    out_ref[:, width:2 * width] = stat
    for t in range(n):
        turn_copy(t, t).wait_recv()
        out_ref[:, t * rows:(t + 1) * rows] = before[t].astype(F32)
    if fold:
        for t in range(n):
            @pl.when(owns(t, s))
            def _():
                mirror_copy(t, t).wait_recv()
                out_ref[:, width + t * rows:width + (t + 1) * rows] = mirrored[t].astype(F32)

            @pl.when(owns(s, t))
            def _():
                mirror_copy(t, t).wait_send()

    for h in range(2):
        shift(h).wait_send()
    own.finish(2)
    follow.finish(4)
    for t in range(n):
        turn_copy(t, t).wait_send()


def reducer(a, b, n, same):
    last = n - 1
    if same:
        return last if b == last else 0 if a == 0 else b
    if a == last or (b == last and a > 0):
        return last
    return 0 if a == 0 or b == 0 else a


def line_kernel(
    nv, n, dosage_ref, class_hbm, effect_hbm, out_ref,
    d_ref, class_ref, effect_ref, after, wt, qt, sq, sq_after, parts,
    wire, near, joined, far, d_wire, d_near, d_joined, d_far, stat_out, stat_in,
    load_sem, d_send, d_recv, near_send, near_recv, far_send, far_recv, stat_send, stat_recv,
):
    depth, width = d_ref.shape
    rows, half = width // n, width // 2
    v, s = lax.axis_index("var"), lax.axis_index("smp")
    nxt, prv = lax.rem(v + 1, nv), lax.rem(v + nv - 1, nv)

    loads = [
        pltpu.make_async_copy(dosage_ref, d_ref, load_sem.at[0]),
        pltpu.make_async_copy(class_hbm, class_ref, load_sem.at[1]),
        pltpu.make_async_copy(effect_hbm, effect_ref, load_sem.at[2]),
    ]
    for load in loads:
        load.start()
    barrier = pltpu.get_barrier_semaphore()
    for beside in (nxt, prv):
        for step in range(n):
            pl.semaphore_signal(barrier, inc=1, device_id=(beside, lax.rem(s + step, n)), device_id_type=MESH)
    for step in range(1, n):
        pl.semaphore_signal(barrier, inc=1, device_id=(v, lax.rem(s + step, n)), device_id_type=MESH)
    for load in loads:
        load.wait()

    own_tiles = [(True, a, b) for a in range(n) for b in range(a, n)]
    after_tiles = [[(False, a, b) for b in range(h * n // 2, (h + 1) * n // 2) for a in range(n)] for h in range(2)]
    number = {}
    for tile in own_tiles + after_tiles[0] + after_tiles[1]:
        if not diagonal(tile):
            number[tile] = len(number)
    order = {tile: at for at, tile in enumerate(own_tiles + after_tiles[0] + after_tiles[1])}

    def at_of(tile):
        return reducer(tile[1], tile[2], n, tile[0])

    def block(index):
        return slice(index * rows, (index + 1) * rows)

    def cols(h):
        return slice(h * half, (h + 1) * half)

    def roles(body):
        for role in range(n):
            pl.when(s == role)(functools.partial(body, role))

    line = lax.broadcasted_iota(jnp.int32, (rows, rows), 0)
    column = lax.broadcasted_iota(jnp.int32, (rows, rows), 1)

    def slot(buffers, tile):
        plain, packed = buffers
        return packed.at[tile[1]] if diagonal(tile) else plain.at[number[tile]]

    def part(tile):
        same, a, b = tile
        first = 0 if same else 2
        x, f = parts[first, block(a), block(b)], parts[first + 1, block(a), block(b)]
        if not diagonal(tile):
            return x, f
        middle = jnp.sum(jnp.where(line == column, f, 0.0), axis=0, keepdims=True)
        return jnp.where(line <= column, x, f), jnp.broadcast_to(middle, (EXTRA, rows))

    def places(tile):
        return (slice(0, rows), slice(rows, rows + EXTRA)) if diagonal(tile) else (0, 1)

    def put(buffers, tile, values):
        for where, value in zip(places(tile), values):
            slot(buffers, tile)[where] = value.astype(BF16)

    def get(buffers, tile):
        return [slot(buffers, tile)[where].astype(F32) for where in places(tile)]

    WIRE, NEAR, JOINED, FAR = (wire, d_wire), (near, d_near), (joined, d_joined), (far, d_far)

    def near_copy(tile, target):
        return pltpu.make_async_remote_copy(
            src_ref=slot(WIRE, tile), dst_ref=slot(NEAR, tile),
            send_sem=near_send.at[order[tile]], recv_sem=near_recv.at[order[tile]],
            device_id=(v, target), device_id_type=MESH,
        )

    def far_copy(tile, target):
        return pltpu.make_async_remote_copy(
            src_ref=slot(JOINED, tile), dst_ref=slot(FAR, tile),
            send_sem=far_send.at[order[tile]], recv_sem=far_recv.at[order[tile]],
            device_id=(v, target), device_id_type=MESH,
        )

    def stat_copy(tile, turned, target, to):
        return pltpu.make_async_remote_copy(
            src_ref=stat_out.at[order[tile], turned], dst_ref=stat_in.at[to],
            send_sem=stat_send.at[order[tile], turned], recv_sem=stat_recv.at[to],
            device_id=target, device_id_type=MESH,
        )

    def shift(h):
        return pltpu.make_async_remote_copy(
            src_ref=d_ref.at[:, cols(h)], dst_ref=after.at[:, cols(h)],
            send_sem=d_send.at[h], recv_sem=d_recv.at[h],
            device_id=(prv, s), device_id_type=MESH,
        )

    def outer(role):
        return role in (0, n - 1)

    def apart(role, tile):
        return role // 2 != at_of(tile) // 2

    def starts(role, tiles):
        sent = [t for t in tiles if at_of(t) != role and (outer(role) or not apart(role, t))]
        return sorted(sent, key=lambda t: not apart(role, t))

    def joins(role, tiles):
        return [] if outer(role) else starts(role ^ 1, [t for t in tiles if apart(role, t)])

    def ends(role, tiles):
        return [t for t in tiles if at_of(t) == role]

    def start(role, tiles):
        for tile in starts(role, tiles):
            put(WIRE, tile, part(tile))
            near_copy(tile, role ^ 1).start()

    def join(role, tile):
        near_copy(tile, role ^ 1).wait_recv()
        put(JOINED, tile, [x + y for x, y in zip(part(tile), get(NEAR, tile))])
        far_copy(tile, at_of(tile)).start()

    def goals(role, tile):
        same, a, b = tile
        if not same:
            return [(0, (v, a), a == role, 2 * n + b), (1, (nxt, b), False, a)]
        return [(0, (v, a), a == role, n + b)] + ([(1, (v, b), b == role, n + a)] if a != b else [])

    def end(role, tile):
        near_copy(tile, role ^ 1).wait_recv()
        far_copy(tile, role ^ 1).wait_recv()
        x, f = [p + q + r for p, q, r in zip(part(tile), get(NEAR, tile), get(FAR, tile))]
        if diagonal(tile):
            packed, middle = x, f[:1]
            mirrored = packed.T
            x = jnp.where(line <= column, packed, mirrored)
            f = jnp.where(line == column, middle, jnp.where(line > column, packed, mirrored))
        stat = x / jnp.sqrt(f + 1e-05)
        for turned, target, local, to in goals(role, tile):
            value = stat.T if turned else stat
            if local:
                out_ref[:, block(to)] = value
            else:
                stat_out[order[tile], turned] = value.astype(BF16)
                stat_copy(tile, turned, target, to).start()

    def weave(*lists):
        keyed = [((at + 1) / (len(steps) + 1), step) for steps in lists for at, step in enumerate(steps)]
        return [step for _, step in sorted(keyed, key=lambda pair: pair[0])]

    classes = effect_ref.shape[0]
    mean = effect_ref[0]
    for c in range(1, classes):
        mean = mean + effect_ref[c]
    mean = mean / classes
    picked = class_ref[...]
    trait = jnp.zeros(picked.shape, F32)
    for c in range(classes):
        trait = jnp.where(picked == c, effect_ref[c] - mean, trait)
    for at in range(0, width, LANES):
        values = d_ref[:, at:at + LANES].astype(F32).T
        wt[at:at + LANES, :] = (values * trait).astype(BF16)
        qt[at:at + LANES, :] = (values * values).astype(BF16)

    def squares(values):
        values = values.astype(F32)
        return (values * values).astype(BF16)

    sq[...] = squares(d_ref[...])
    for h in range(2):
        parts[0, cols(h), h * half:] = jnp.dot(wt[cols(h), :], d_ref[:, h * half:], preferred_element_type=F32)
        parts[1, cols(h), h * half:] = jnp.dot(qt[cols(h), :], sq[:, h * half:], preferred_element_type=F32)
    pl.semaphore_wait(barrier, 3 * n - 1)
    for h in range(2):
        shift(h).start()
    roles(lambda role: start(role, own_tiles))

    def follow(h):
        shift(h).wait_recv()
        sq_after[:, cols(h)] = squares(after[:, cols(h)])
        parts[2, :, cols(h)] = jnp.dot(wt[...], after[:, cols(h)], preferred_element_type=F32)
        parts[3, :, cols(h)] = jnp.dot(qt[...], sq_after[:, cols(h)], preferred_element_type=F32)
        roles(lambda role: start(role, after_tiles[h]))

    follow(0)

    def join_own(role):
        for tile in joins(role, own_tiles):
            join(role, tile)

    roles(join_own)
    follow(1)

    def rest(role):
        def steps(act, tiles):
            return [functools.partial(act, role, tile) for tile in tiles]

        first = weave(steps(join, joins(role, after_tiles[0])), steps(end, ends(role, own_tiles)))
        second = weave(steps(join, joins(role, after_tiles[1])), steps(end, ends(role, after_tiles[0])))
        for step in first + second + steps(end, ends(role, after_tiles[1])):
            step()

    roles(rest)

    def close(role):
        every = own_tiles + after_tiles[0] + after_tiles[1]
        for tile in sorted(every, key=lambda t: order[t]):
            for turned, target, local, to in goals(at_of(tile), tile):
                here = tile[2] if turned else tile[1]
                if here == role and not local:
                    arrived = pltpu.make_async_remote_copy(
                        src_ref=stat_in.at[to], dst_ref=stat_in.at[to],
                        send_sem=stat_send.at[0, 0], recv_sem=stat_recv.at[to],
                        device_id=(v, role ^ 1), device_id_type=MESH,
                    )
                    arrived.wait_recv()
                    out_ref[:, block(to)] = stat_in[to].astype(F32)
        for tile in starts(role, every):
            near_copy(tile, role ^ 1).wait_send()
        for tile in joins(role, every):
            far_copy(tile, at_of(tile)).wait_send()
        for tile in ends(role, every):
            for turned, target, local, to in goals(role, tile):
                if not local:
                    stat_copy(tile, turned, target, to).wait_send()

    roles(close)
    for h in range(2):
        shift(h).wait_send()


def diagonal(tile):
    return tile[0] and tile[1] == tile[2]


def solution(mesh):
    nv, n = mesh.shape["var"], mesh.shape["smp"]

    def shards(dosage, trait_class, class_effect):
        depth, width = dosage.shape
        rows, half, pairs = width // n, width // 2, n // 2
        dma, vmem = pltpu.SemaphoreType.DMA, pltpu.VMEM

        def call(body, scratch):
            return pl.pallas_call(
                functools.partial(body, nv, n),
                out_shape=jax.ShapeDtypeStruct((rows, 3 * width), F32),
                in_specs=[pl.BlockSpec(memory_space=pltpu.HBM)] * 3,
                out_specs=pl.BlockSpec(memory_space=vmem),
                scratch_shapes=[
                    vmem((depth, width), BF16),
                    vmem((1, depth), jnp.int32),
                    pltpu.SMEM(class_effect.shape, F32),
                    vmem((depth, width), BF16),
                    vmem((width, depth), BF16),
                    vmem((width, depth), BF16),
                    vmem((depth, width), BF16),
                    *scratch,
                ],
                compiler_params=pltpu.CompilerParams(
                    collective_id=0, has_side_effects=True, vmem_limit_bytes=32 * 1024 * 1024
                ),
            )(*(pltpu.with_memory_space_constraint(x, pltpu.HBM) for x in (dosage, trait_class.reshape(1, depth), class_effect)))

        if n == 4 and rows % LANES == 0:
            tiles = n * (n + 1) // 2 + n * n
            return call(line_kernel, [
                vmem((depth, width), BF16),
                vmem((4, width, width), F32),
                *[vmem((tiles - n, 2, rows, rows), BF16)] * 4,
                *[vmem((n, rows + EXTRA, rows), BF16)] * 4,
                vmem((tiles, 2, rows, rows), BF16),
                vmem((3 * n, rows, rows), BF16),
                dma((3,)), dma((2,)), dma((2,)),
                *[dma((tiles,))] * 4,
                dma((tiles, 2)), dma((3 * n,)),
            ])

        def buffers(units, wide):
            return [
                vmem((units, width, wide), F32),
                vmem((units, width, wide), BF16),
                vmem((units, pairs, 2, rows, wide), BF16),
                vmem((units, pairs, 2, rows, wide), BF16),
                vmem((units, pairs, rows, wide), BF16),
                vmem((units, rows, wide), BF16),
            ]

        def semaphores(units):
            return [
                dma((units, pairs, 2)), dma((units, pairs, 2)), dma((units, pairs, 2)),
                dma((units, pairs)), dma((units,)), dma((units,)),
            ]

        return call(kernel, [
            vmem((width, rows), BF16),
            vmem((n, rows, rows), BF16),
            vmem((width, rows), BF16),
            vmem((n, rows, rows), BF16),
            *buffers(2, width),
            *buffers(4, half),
            dma((3,)), dma((2,)), dma((2,)),
            dma((n,)), dma((n,)), dma((n,)), dma((n,)),
            *semaphores(2),
            *semaphores(4),
        ])

    in_specs = (P("smp", "var"), P("smp"), P())
    out_specs = P(("var", "smp"), None)
    return jax.shard_map(shards, mesh=mesh, in_specs=in_specs, out_specs=out_specs, check_vma=False)
```

```python
import functools

import jax
import jax.numpy as jnp
from jax import lax
from jax.experimental import pallas as pl
from jax.experimental.pallas import tpu as pltpu
from jax.sharding import PartitionSpec as P

MESH = pl.DeviceIdType.MESH
F32, BF16 = jnp.float32, jnp.bfloat16
LANES = 128
EXTRA = 16


def kernel(
    nv, n, dosage_ref, class_hbm, effect_hbm, out_ref,
    d_ref, class_ref, effect_ref, after, wt, qt, sq, turned, before, own_turned, mirrored,
    own_part, own_wire, own_relay, own_fwd, own_summed, own_direct,
    next_part, next_wire, next_relay, next_fwd, next_summed, next_direct,
    load_sem, d_send, d_recv, t_send, t_recv, m_send, m_recv,
    own_rs, own_rr, own_fs, own_sr, own_ds, own_dr,
    next_rs, next_rr, next_fs, next_sr, next_ds, next_dr,
):
    depth, width = d_ref.shape
    rows, half, pairs = width // n, width // 2, n // 2
    fold = rows % LANES == 0
    v, s = lax.axis_index("var"), lax.axis_index("smp")
    nxt, prv = lax.rem(v + 1, nv), lax.rem(v + nv - 1, nv)
    pair, odd = s // 2, lax.rem(s, 2)
    partner = s + 1 - 2 * odd

    loads = [
        pltpu.make_async_copy(dosage_ref, d_ref, load_sem.at[0]),
        pltpu.make_async_copy(class_hbm, class_ref, load_sem.at[1]),
        pltpu.make_async_copy(effect_hbm, effect_ref, load_sem.at[2]),
    ]
    for load in loads:
        load.start()
    barrier = pltpu.get_barrier_semaphore()
    for near in (nxt, prv):
        for step in range(n):
            pl.semaphore_signal(barrier, inc=1, device_id=(near, lax.rem(s + step, n)), device_id_type=MESH)
    for step in range(1, n):
        pl.semaphore_signal(barrier, inc=1, device_id=(v, lax.rem(s + step, n)), device_id_type=MESH)
    for load in loads:
        load.wait()

    def cols(h):
        return slice(h * half, (h + 1) * half)

    def shift(h):
        return pltpu.make_async_remote_copy(
            src_ref=d_ref.at[:, cols(h)], dst_ref=after.at[:, cols(h)],
            send_sem=d_send.at[h], recv_sem=d_recv.at[h],
            device_id=(prv, s), device_id_type=MESH,
        )

    classes = effect_ref.shape[0]
    mean = effect_ref[0]
    for c in range(1, classes):
        mean = mean + effect_ref[c]
    mean = mean / classes
    picked = class_ref[...]
    trait = jnp.zeros(picked.shape, F32)
    for c in range(classes):
        trait = jnp.where(picked == c, effect_ref[c] - mean, trait)
    for at in range(0, width, LANES):
        values = d_ref[:, at:at + LANES].astype(F32).T
        wt[at:at + LANES, :] = (values * trait).astype(BF16)
        qt[at:at + LANES, :] = (values * values).astype(BF16)

    def owns(a, c):
        from_a, from_c = abs_of(2 * a - (n - 1)), abs_of(2 * c - (n - 1))
        return jnp.logical_or(from_a > from_c, jnp.logical_and(from_a == from_c, a < c))

    def abs_of(x):
        return lax.max(x, -x) if isinstance(x, jax.Array) else jnp.int32(abs(x))

    def extent(t):
        if not fold:
            return slice(0, width)
        first, last = (t, n - 1 - t) if t < pairs else (n - t, t)
        return slice(first * rows, (last + 1) * rows)

    def cases(index, count, body):
        for known in range(count):
            pl.when(index == known)(functools.partial(body, known))

    def at_rows(index):
        return pl.ds(pl.multiple_of(index * rows, rows), rows)

    def outer(k):
        higher = lax.rem(pair + k, pairs) > pair
        return jnp.logical_or(
            jnp.logical_and(higher, odd == 0), jnp.logical_and(jnp.logical_not(higher), odd == 1)
        )

    class Group:
        def __init__(self, folded, part, wire, relay, fwd, summed, direct, rs, rr, fs, sr, ds, dr):
            self.folded, self.part, self.wire, self.relay = folded, part, wire, relay
            self.fwd, self.summed, self.direct = fwd, summed, direct
            self.rs, self.rr, self.fs, self.sr, self.ds, self.dr = rs, rr, fs, sr, ds, dr

        def span(self, t):
            return extent(t) if self.folded else slice(None)

        def by(self, index, count, body):
            if self.folded:
                cases(index, count, body)
            else:
                body(index)

        def relay_copy(self, u, other, j):
            t = 2 * other + j
            span = self.span(t)
            return pltpu.make_async_remote_copy(
                src_ref=self.wire.at[u, at_rows(t), span], dst_ref=self.relay.at[u, other, j, :, span],
                send_sem=self.rs.at[u, other, j], recv_sem=self.rr.at[u, other, j],
                device_id=(v, partner), device_id_type=MESH,
            )

        def fwd_copy(self, u, other, j):
            t = 2 * other + j
            span = self.span(t)
            return pltpu.make_async_remote_copy(
                src_ref=self.fwd.at[u, other, j, :, span], dst_ref=self.summed.at[u, pair, :, span],
                send_sem=self.fs.at[u, other, j], recv_sem=self.sr.at[u, pair],
                device_id=(v, t), device_id_type=MESH,
            )

        def sum_wait(self, u, source, t):
            span = self.span(t)
            here = self.summed.at[u, source, :, span]
            pltpu.make_async_remote_copy(
                src_ref=here, dst_ref=here, send_sem=self.fs.at[u, source, 0], recv_sem=self.sr.at[u, source],
                device_id=(v, partner), device_id_type=MESH,
            ).wait_recv()

        def dir_copy(self, u, t):
            span = self.span(t)
            return pltpu.make_async_remote_copy(
                src_ref=self.wire.at[u, at_rows(t), span], dst_ref=self.direct.at[u, :, span],
                send_sem=self.ds.at[u], recv_sem=self.dr.at[u],
                device_id=(v, partner), device_id_type=MESH,
            )

        def product(self, u, left, right):
            got = jnp.dot(left[...], right, preferred_element_type=F32)
            self.part[u] = got
            self.wire[u] = got.astype(BF16)

        def send_relays(self, u):
            for k in range(1, pairs):
                @pl.when(outer(k))
                def _():
                    def send(other):
                        for j in range(2):
                            self.relay_copy(u, other, j).start()

                    self.by(lax.rem(pair + k, pairs), pairs, send)

        def send_sums(self, u):
            for k in range(1, pairs):
                @pl.when(jnp.logical_not(outer(k)))
                def _():
                    def send(other):
                        for j in range(2):
                            self.relay_copy(u, other, j).wait_recv()
                            own = self.part[u, at_rows(2 * other + j), :]
                            self.fwd[u, other, j] = (own + self.relay[u, other, j].astype(F32)).astype(BF16)
                            self.fwd_copy(u, other, j).start()

                    self.by(lax.rem(pair + k, pairs), pairs, send)

        def send_direct(self, u):
            self.by(partner, n, lambda t: self.dir_copy(u, t).start())

        def total(self, u):
            def wait(t):
                self.dir_copy(u, t).wait_recv()
                for k in range(1, pairs):
                    self.sum_wait(u, lax.rem(pair + k, pairs), t)

            self.by(s, n, wait)
            got = self.part[u, at_rows(s), :] + self.direct[u].astype(F32)
            for k in range(1, pairs):
                got = got + self.summed[u, lax.rem(pair + k, pairs)].astype(F32)
            return got

        def finish(self, units):
            for u in range(units):
                self.by(partner, n, lambda t: self.dir_copy(u, t).wait_send())
                for k in range(1, pairs):
                    def relays(other):
                        for j in range(2):
                            self.relay_copy(u, other, j).wait_send()

                    def sums(other):
                        for j in range(2):
                            self.fwd_copy(u, other, j).wait_send()

                    other = lax.rem(pair + k, pairs)

                    @pl.when(outer(k))
                    def _():
                        self.by(other, pairs, relays)

                    @pl.when(jnp.logical_not(outer(k)))
                    def _():
                        self.by(other, pairs, sums)

    own = Group(
        fold, own_part, own_wire, own_relay, own_fwd, own_summed, own_direct,
        own_rs, own_rr, own_fs, own_sr, own_ds, own_dr,
    )
    follow = Group(
        False, next_part, next_wire, next_relay, next_fwd, next_summed, next_direct,
        next_rs, next_rr, next_fs, next_sr, next_ds, next_dr,
    )

    def squares(values):
        values = values.astype(F32)
        return (values * values).astype(BF16)

    own.product(0, wt, d_ref[...])
    pl.semaphore_wait(barrier, 3 * n - 1)
    for h in range(2):
        shift(h).start()
    own.send_relays(0)
    sq[...] = squares(d_ref[...])
    own.product(1, qt, sq[...])
    own.send_relays(1)
    late = outer(1) if pairs > 1 else jnp.logical_and(odd == 0, odd == 1)

    for u in range(2):
        own.send_direct(u)
    for h in range(2):
        shift(h).wait_recv()
        follow.product(2 * h, wt, after[:, cols(h)])
        follow.send_relays(2 * h)
        sq[:, cols(h)] = squares(after[:, cols(h)])
        follow.product(2 * h + 1, qt, sq[:, cols(h)])
        follow.send_relays(2 * h + 1)

        @pl.when(jnp.logical_not(late))
        def _():
            for u in range(2 * h, 2 * h + 2):
                follow.send_direct(u)

        if h == 0:
            for u in range(2):
                own.send_sums(u)

    @pl.when(late)
    def _():
        for u in range(4):
            follow.send_direct(u)

    for u in range(4):
        follow.send_sums(u)

    def turn_copy(t, slot):
        return pltpu.make_async_remote_copy(
            src_ref=turned.at[t * rows:(t + 1) * rows], dst_ref=before.at[slot],
            send_sem=t_send.at[t], recv_sem=t_recv.at[slot],
            device_id=(nxt, t), device_id_type=MESH,
        )

    def mirror_copy(t, slot):
        return pltpu.make_async_remote_copy(
            src_ref=own_turned.at[t * rows:(t + 1) * rows], dst_ref=mirrored.at[slot],
            send_sem=m_send.at[t], recv_sem=m_recv.at[slot],
            device_id=(v, t), device_id_type=MESH,
        )

    for h in range(2):
        stat = follow.total(2 * h) / jnp.sqrt(follow.total(2 * h + 1) + 1e-05)
        out_ref[:, 2 * width + h * half:2 * width + (h + 1) * half] = stat
        turned[cols(h), :] = stat.T.astype(BF16)
        for t in range(h * pairs, (h + 1) * pairs):
            turn_copy(t, s).start()
    stat = own.total(0) / jnp.sqrt(own.total(1) + 1e-05)
    if fold:
        own_turned[...] = stat.T.astype(BF16)
        for t in range(n):
            @pl.when(owns(s, t))
            def _():
                mirror_copy(t, s).start()
    out_ref[:, width:2 * width] = stat
    for t in range(n):
        turn_copy(t, t).wait_recv()
        out_ref[:, t * rows:(t + 1) * rows] = before[t].astype(F32)
    if fold:
        for t in range(n):
            @pl.when(owns(t, s))
            def _():
                mirror_copy(t, t).wait_recv()
                out_ref[:, width + t * rows:width + (t + 1) * rows] = mirrored[t].astype(F32)

            @pl.when(owns(s, t))
            def _():
                mirror_copy(t, t).wait_send()

    for h in range(2):
        shift(h).wait_send()
    own.finish(2)
    follow.finish(4)
    for t in range(n):
        turn_copy(t, t).wait_send()


REDUCER = (0, 0, 0, 3, 1, 2, 3, 2, 3, 3, 0, 0, 0, 3, 0, 1, 1, 3, 0, 2, 2, 3, 3, 3, 3, 3)
PLAN = (
    (3, 6, 8, 9, 5, 7, 4, -1, 22, 13, 17, 21, 25, -2, 23, 24, 19, 20, 15, 16, 0, 1, 2, 10, 14, 18, 11, 12),
    (3, 6, 8, 9, 5, 7, 4, -1, 22, 13, 17, 21, 25, -2, 23, 24, 19, 20, 15, 16, 0, 1, 2, 10, 14, 18, 11, 12),
    (3, 6, 8, 9, 5, 7, 0, -1, 22, 13, 1, 17, 2, 21, 4, 25, -2, 23, 10, 24, 14, 18, 19, 11, 12, 20, 15, 16),
    (3, 6, 8, 9, 5, 7, 0, 1, 2, 4, -1, 22, 13, 17, 21, 25, 10, -2, 23, 24, 14, 19, 20, 18, 11, 12, 15, 16),
    (0, 1, 3, 2, 4, 6, 8, 9, -1, 10, 5, 14, 7, 18, 22, -2, 11, 13, 12, 17, 15, 21, 16, 25, 23, 24, 19, 20),
    (0, 3, 1, 6, 2, 8, 4, 9, 5, 7, -1, 10, 22, 13, 14, 18, 17, 21, -2, 11, 25, 12, 23, 15, 16, 24, 19, 20),
    (0, 1, 2, 4, 5, 7, -1, 10, 14, 18, -2, 11, 12, 15, 16, 19, 20, 3, 6, 8, 9, 22, 13, 17, 21, 25, 23, 24),
    (0, 1, 2, 4, 5, 7, -1, 10, 14, 18, -2, 11, 12, 15, 16, 19, 20, 3, 6, 8, 9, 22, 13, 17, 21, 25, 23, 24),
)


def line_kernel(
    nv, n, dosage_ref, class_hbm, effect_hbm, out_ref,
    d_ref, class_ref, effect_ref, after, wt, qt, sq, sq_after, dt, w_after, trait_column, parts,
    wire, near, joined, far, d_wire, d_near, d_joined, d_far, stat_out, stat_in,
    open_sem, load_sem, d_send, d_recv, near_send, near_recv, far_send, far_recv, stat_send, stat_recv,
):
    depth, width = d_ref.shape
    rows, half = width // n, width // 2
    v, s = lax.axis_index("var"), lax.axis_index("smp")
    nxt, prv = lax.rem(v + 1, nv), lax.rem(v + nv - 1, nv)

    loads = [
        pltpu.make_async_copy(dosage_ref, d_ref, load_sem.at[0]),
        pltpu.make_async_copy(class_hbm, class_ref, load_sem.at[1]),
        pltpu.make_async_copy(effect_hbm, effect_ref, load_sem.at[2]),
    ]
    for load in loads:
        load.start()
    barrier = pltpu.get_barrier_semaphore()
    host = n - 1

    def greet(target):
        pl.semaphore_signal(barrier, inc=1, device_id=target, device_id_type=MESH)

    greet((nxt, s))
    greet((prv, host))
    for role in range(n):
        @pl.when(s == role)
        def _():
            for other in {role - 1, role + 1, host} - {-1, n, role}:
                greet((v, other))

    for load in loads:
        load.wait()

    tiles = [(True, a, b) for a in range(n) for b in range(a, n)] + [(False, a, b) for a in range(n) for b in range(n)]
    order = {tile: at for at, tile in enumerate(tiles)}
    number = {tile: at for at, tile in enumerate(t for t in tiles if not diagonal(t))}
    spread = [b for h in range(n // 2) for b in (h, n - 1 - h)]

    def at_of(tile):
        return REDUCER[order[tile]]

    def block(index):
        return slice(index * rows, (index + 1) * rows)

    def cols(h):
        return slice(h * half, (h + 1) * half)

    def roles(body):
        for role in range(n):
            pl.when(s == role)(functools.partial(body, role))

    def plans(body):
        for at in range(2 * n):
            pl.when(2 * s + lax.rem(v, 2) == at)(functools.partial(body, at // 2, PLAN[at]))

    line = lax.broadcasted_iota(jnp.int32, (rows, rows), 0)
    column = lax.broadcasted_iota(jnp.int32, (rows, rows), 1)

    def slot(buffers, tile):
        plain, packed = buffers
        return packed.at[tile[1]] if diagonal(tile) else plain.at[number[tile]]

    def part(tile):
        same, a, b = tile
        first = 0 if same else 2
        b = b if same else spread.index(b)
        x, f = parts[first, block(a), block(b)], parts[first + 1, block(a), block(b)]
        if not diagonal(tile):
            return x, f
        middle = jnp.sum(jnp.where(line == column, f, 0.0), axis=0, keepdims=True)
        return jnp.where(line <= column, x, f), jnp.broadcast_to(middle, (EXTRA, rows))

    def places(tile):
        return (slice(0, rows), slice(rows, rows + EXTRA)) if diagonal(tile) else (0, 1)

    def put(buffers, tile, values):
        for where, value in zip(places(tile), values):
            slot(buffers, tile)[where] = value.astype(BF16)

    def get(buffers, tile):
        return [slot(buffers, tile)[where].astype(F32) for where in places(tile)]

    WIRE, NEAR, JOINED, FAR = (wire, d_wire), (near, d_near), (joined, d_joined), (far, d_far)

    def near_copy(tile, target):
        return pltpu.make_async_remote_copy(
            src_ref=slot(WIRE, tile), dst_ref=slot(NEAR, tile),
            send_sem=near_send.at[order[tile]], recv_sem=near_recv.at[order[tile]],
            device_id=(v, target), device_id_type=MESH,
        )

    def far_copy(tile, target):
        return pltpu.make_async_remote_copy(
            src_ref=slot(JOINED, tile), dst_ref=slot(FAR, tile),
            send_sem=far_send.at[order[tile]], recv_sem=far_recv.at[order[tile]],
            device_id=(v, target), device_id_type=MESH,
        )

    def stat_copy(tile, turned, target, to):
        return pltpu.make_async_remote_copy(
            src_ref=stat_out.at[order[tile], turned], dst_ref=stat_in.at[to],
            send_sem=stat_send.at[order[tile], turned], recv_sem=stat_recv.at[to],
            device_id=target, device_id_type=MESH,
        )

    def shift(at):
        return pltpu.make_async_remote_copy(
            src_ref=d_ref.at[:, block(spread[at])], dst_ref=after.at[:, block(at)],
            send_sem=d_send.at[at], recv_sem=d_recv.at[at],
            device_id=(prv, s), device_id_type=MESH,
        )

    def outer(role):
        return role in (0, n - 1)

    def kind(role, tile):
        target = at_of(tile)
        if target == role:
            return end
        if outer(role):
            return start
        return hand_on if target == role ^ 1 else join

    def mine(role, *acts):
        return [tile for tile in tiles if kind(role, tile) in acts]

    def start(role, tile):
        put(WIRE, tile, part(tile))
        near_copy(tile, role ^ 1).start()

    def join(role, tile):
        near_copy(tile, role ^ 1).wait_recv()
        put(JOINED, tile, [x + y for x, y in zip(part(tile), get(NEAR, tile))])
        far_copy(tile, n - 1 - role).start()

    def hand_on(role, tile):
        far_copy(tile, n - 1 - role).wait_recv()
        put(WIRE, tile, [x + y for x, y in zip(part(tile), get(FAR, tile))])
        near_copy(tile, role ^ 1).start()

    def goals(role, tile):
        same, a, b = tile
        if not same:
            return [(0, (v, a), a == role, 2 * n + b), (1, (nxt, b), False, a)]
        return [(0, (v, a), a == role, n + b)] + ([(1, (v, b), b == role, n + a)] if a != b else [])

    def end(role, tile):
        near_copy(tile, role ^ 1).wait_recv()
        x, f = [p + q for p, q in zip(part(tile), get(NEAR, tile))]
        if not outer(role):
            far_copy(tile, n - 1 - role).wait_recv()
            x, f = [p + q for p, q in zip((x, f), get(FAR, tile))]
        if diagonal(tile):
            packed, middle = x, f[:1]
            mirrored = packed.T
            x = jnp.where(line <= column, packed, mirrored)
            f = jnp.where(line == column, middle, jnp.where(line > column, packed, mirrored))
        stat = x / jnp.sqrt(f + 1e-05)
        for turned, target, local, to in goals(role, tile):
            value = stat.T if turned else stat
            if local:
                out_ref[:, block(to)] = value
            else:
                stat_out[order[tile], turned] = value.astype(BF16)
                stat_copy(tile, turned, target, to).start()

    classes = effect_ref.shape[0]
    mean = effect_ref[0]
    for c in range(1, classes):
        mean = mean + effect_ref[c]
    mean = mean / classes
    picked = class_ref[...]
    trait = jnp.zeros(picked.shape, F32)
    for c in range(classes):
        trait = jnp.where(picked == c, effect_ref[c] - mean, trait)
    for at in range(0, width, LANES):
        values = d_ref[:, at:at + LANES].astype(F32).T
        wt[at:at + LANES, :] = (values * trait).astype(BF16)
        qt[at:at + LANES, :] = (values * values).astype(BF16)
        dt[at:at + LANES, :] = values.astype(BF16)
    trait_column[...] = jnp.broadcast_to(trait, (LANES, depth)).T

    def squares(values):
        values = values.astype(F32)
        return (values * values).astype(BF16)

    sq[...] = squares(d_ref[...])
    for h in range(2):
        parts[0, cols(h), h * half:] = jnp.dot(wt[cols(h), :], d_ref[:, h * half:], preferred_element_type=F32)
        parts[1, cols(h), h * half:] = jnp.dot(qt[cols(h), :], sq[:, h * half:], preferred_element_type=F32)

    def enter(role):
        if role != host:
            pl.semaphore_wait(barrier, len({role - 1, role + 1} - {-1}) + 1)
        else:
            pl.semaphore_wait(barrier, 2 * n)
            for other in range(host):
                pl.semaphore_signal(open_sem, inc=1, device_id=(v, other), device_id_type=MESH)

    def run(stage):
        def body(role, plan):
            marks = [-1] + [plan.index(-1 - h) for h in range(2)] + [len(plan)]
            first_end = [at for at in plan if at >= 0 and kind(role, tiles[at]) is end][0]
            for at in plan[marks[stage] + 1:marks[stage + 1]]:
                if at == first_end and role != host:
                    pl.semaphore_wait(open_sem, 1)
                kind(role, tiles[at])(role, tiles[at])

        plans(body)

    def follow(h):
        for at in range(h * n // 2, (h + 1) * n // 2):
            shift(at).wait_recv()
        sq_after[:, cols(h)] = squares(after[:, cols(h)])
        for at in range(h * half, (h + 1) * half, LANES):
            w_after[:, at:at + LANES] = (after[:, at:at + LANES].astype(F32) * trait_column[...]).astype(BF16)
        cross = jnp.dot(wt[...], after[:, cols(h)], preferred_element_type=F32)
        cross = cross + jnp.dot(dt[...], w_after[:, cols(h)], preferred_element_type=F32)
        parts[2, :, cols(h)] = 0.5 * cross
        parts[3, :, cols(h)] = jnp.dot(qt[...], sq_after[:, cols(h)], preferred_element_type=F32)

    roles(enter)
    for at in range(n):
        shift(at).start()
    run(0)
    follow(0)
    run(1)
    follow(1)
    run(2)

    def close(role):
        for tile in tiles:
            for turned, target, local, to in goals(at_of(tile), tile):
                here = tile[2] if turned else tile[1]
                if here == role and not local:
                    arrived = pltpu.make_async_remote_copy(
                        src_ref=stat_in.at[to], dst_ref=stat_in.at[to],
                        send_sem=stat_send.at[0, 0], recv_sem=stat_recv.at[to],
                        device_id=(v, role ^ 1), device_id_type=MESH,
                    )
                    arrived.wait_recv()
                    out_ref[:, block(to)] = stat_in[to].astype(F32)
        for tile in mine(role, start, hand_on):
            near_copy(tile, role ^ 1).wait_send()
        for tile in mine(role, join):
            far_copy(tile, n - 1 - role).wait_send()
        for tile in mine(role, end):
            for turned, target, local, to in goals(role, tile):
                if not local:
                    stat_copy(tile, turned, target, to).wait_send()

    roles(close)
    for at in range(n):
        shift(at).wait_send()


def diagonal(tile):
    return tile[0] and tile[1] == tile[2]


def solution(mesh):
    nv, n = mesh.shape["var"], mesh.shape["smp"]

    def shards(dosage, trait_class, class_effect):
        depth, width = dosage.shape
        rows, half, pairs = width // n, width // 2, n // 2
        dma, vmem = pltpu.SemaphoreType.DMA, pltpu.VMEM

        def call(body, scratch):
            return pl.pallas_call(
                functools.partial(body, nv, n),
                out_shape=jax.ShapeDtypeStruct((rows, 3 * width), F32),
                in_specs=[pl.BlockSpec(memory_space=pltpu.HBM)] * 3,
                out_specs=pl.BlockSpec(memory_space=vmem),
                scratch_shapes=[
                    vmem((depth, width), BF16),
                    vmem((1, depth), jnp.int32),
                    pltpu.SMEM(class_effect.shape, F32),
                    vmem((depth, width), BF16),
                    vmem((width, depth), BF16),
                    vmem((width, depth), BF16),
                    vmem((depth, width), BF16),
                    *scratch,
                ],
                compiler_params=pltpu.CompilerParams(
                    collective_id=0, has_side_effects=True, vmem_limit_bytes=32 * 1024 * 1024
                ),
            )(*(pltpu.with_memory_space_constraint(x, pltpu.HBM) for x in (dosage, trait_class.reshape(1, depth), class_effect)))

        if n == 4 and rows % LANES == 0:
            tiles = n * (n + 1) // 2 + n * n
            return call(line_kernel, [
                vmem((depth, width), BF16),
                vmem((width, depth), BF16),
                vmem((depth, width), BF16),
                vmem((depth, LANES), F32),
                vmem((4, width, width), F32),
                *[vmem((tiles - n, 2, rows, rows), BF16)] * 4,
                *[vmem((n, rows + EXTRA, rows), BF16)] * 4,
                vmem((tiles, 2, rows, rows), BF16),
                vmem((3 * n, rows, rows), BF16),
                pltpu.SemaphoreType.REGULAR,
                dma((3,)), dma((n,)), dma((n,)),
                *[dma((tiles,))] * 4,
                dma((tiles, 2)), dma((3 * n,)),
            ])

        def buffers(units, wide):
            return [
                vmem((units, width, wide), F32),
                vmem((units, width, wide), BF16),
                vmem((units, pairs, 2, rows, wide), BF16),
                vmem((units, pairs, 2, rows, wide), BF16),
                vmem((units, pairs, rows, wide), BF16),
                vmem((units, rows, wide), BF16),
            ]

        def semaphores(units):
            return [
                dma((units, pairs, 2)), dma((units, pairs, 2)), dma((units, pairs, 2)),
                dma((units, pairs)), dma((units,)), dma((units,)),
            ]

        return call(kernel, [
            vmem((width, rows), BF16),
            vmem((n, rows, rows), BF16),
            vmem((width, rows), BF16),
            vmem((n, rows, rows), BF16),
            *buffers(2, width),
            *buffers(4, half),
            dma((3,)), dma((2,)), dma((2,)),
            dma((n,)), dma((n,)), dma((n,)), dma((n,)),
            *semaphores(2),
            *semaphores(4),
        ])

    in_specs = (P("smp", "var"), P("smp"), P())
    out_specs = P(("var", "smp"), None)
    return jax.shard_map(shards, mesh=mesh, in_specs=in_specs, out_specs=out_specs, check_vma=False)
```

```python
import functools

import jax
import jax.numpy as jnp
from jax import lax
from jax.experimental import pallas as pl
from jax.experimental.pallas import tpu as pltpu
from jax.sharding import PartitionSpec as P

MESH = pl.DeviceIdType.MESH
F32, BF16 = jnp.float32, jnp.bfloat16
LANES = 128
EXTRA = 16


def kernel(
    nv, n, dosage_ref, class_hbm, effect_hbm, out_ref,
    d_ref, class_ref, effect_ref, after, wt, qt, sq, turned, before, own_turned, mirrored,
    own_part, own_wire, own_relay, own_fwd, own_summed, own_direct,
    next_part, next_wire, next_relay, next_fwd, next_summed, next_direct,
    load_sem, d_send, d_recv, t_send, t_recv, m_send, m_recv,
    own_rs, own_rr, own_fs, own_sr, own_ds, own_dr,
    next_rs, next_rr, next_fs, next_sr, next_ds, next_dr,
):
    depth, width = d_ref.shape
    rows, half, pairs = width // n, width // 2, n // 2
    fold = rows % LANES == 0
    v, s = lax.axis_index("var"), lax.axis_index("smp")
    nxt, prv = lax.rem(v + 1, nv), lax.rem(v + nv - 1, nv)
    pair, odd = s // 2, lax.rem(s, 2)
    partner = s + 1 - 2 * odd

    loads = [
        pltpu.make_async_copy(dosage_ref, d_ref, load_sem.at[0]),
        pltpu.make_async_copy(class_hbm, class_ref, load_sem.at[1]),
        pltpu.make_async_copy(effect_hbm, effect_ref, load_sem.at[2]),
    ]
    for load in loads:
        load.start()
    barrier = pltpu.get_barrier_semaphore()
    for near in (nxt, prv):
        for step in range(n):
            pl.semaphore_signal(barrier, inc=1, device_id=(near, lax.rem(s + step, n)), device_id_type=MESH)
    for step in range(1, n):
        pl.semaphore_signal(barrier, inc=1, device_id=(v, lax.rem(s + step, n)), device_id_type=MESH)
    for load in loads:
        load.wait()

    def cols(h):
        return slice(h * half, (h + 1) * half)

    def shift(h):
        return pltpu.make_async_remote_copy(
            src_ref=d_ref.at[:, cols(h)], dst_ref=after.at[:, cols(h)],
            send_sem=d_send.at[h], recv_sem=d_recv.at[h],
            device_id=(prv, s), device_id_type=MESH,
        )

    classes = effect_ref.shape[0]
    mean = effect_ref[0]
    for c in range(1, classes):
        mean = mean + effect_ref[c]
    mean = mean / classes
    picked = class_ref[...]
    trait = jnp.zeros(picked.shape, F32)
    for c in range(classes):
        trait = jnp.where(picked == c, effect_ref[c] - mean, trait)
    for at in range(0, width, LANES):
        values = d_ref[:, at:at + LANES].astype(F32).T
        wt[at:at + LANES, :] = (values * trait).astype(BF16)
        qt[at:at + LANES, :] = (values * values).astype(BF16)

    def owns(a, c):
        from_a, from_c = abs_of(2 * a - (n - 1)), abs_of(2 * c - (n - 1))
        return jnp.logical_or(from_a > from_c, jnp.logical_and(from_a == from_c, a < c))

    def abs_of(x):
        return lax.max(x, -x) if isinstance(x, jax.Array) else jnp.int32(abs(x))

    def extent(t):
        if not fold:
            return slice(0, width)
        first, last = (t, n - 1 - t) if t < pairs else (n - t, t)
        return slice(first * rows, (last + 1) * rows)

    def cases(index, count, body):
        for known in range(count):
            pl.when(index == known)(functools.partial(body, known))

    def at_rows(index):
        return pl.ds(pl.multiple_of(index * rows, rows), rows)

    def outer(k):
        higher = lax.rem(pair + k, pairs) > pair
        return jnp.logical_or(
            jnp.logical_and(higher, odd == 0), jnp.logical_and(jnp.logical_not(higher), odd == 1)
        )

    class Group:
        def __init__(self, folded, part, wire, relay, fwd, summed, direct, rs, rr, fs, sr, ds, dr):
            self.folded, self.part, self.wire, self.relay = folded, part, wire, relay
            self.fwd, self.summed, self.direct = fwd, summed, direct
            self.rs, self.rr, self.fs, self.sr, self.ds, self.dr = rs, rr, fs, sr, ds, dr

        def span(self, t):
            return extent(t) if self.folded else slice(None)

        def by(self, index, count, body):
            if self.folded:
                cases(index, count, body)
            else:
                body(index)

        def relay_copy(self, u, other, j):
            t = 2 * other + j
            span = self.span(t)
            return pltpu.make_async_remote_copy(
                src_ref=self.wire.at[u, at_rows(t), span], dst_ref=self.relay.at[u, other, j, :, span],
                send_sem=self.rs.at[u, other, j], recv_sem=self.rr.at[u, other, j],
                device_id=(v, partner), device_id_type=MESH,
            )

        def fwd_copy(self, u, other, j):
            t = 2 * other + j
            span = self.span(t)
            return pltpu.make_async_remote_copy(
                src_ref=self.fwd.at[u, other, j, :, span], dst_ref=self.summed.at[u, pair, :, span],
                send_sem=self.fs.at[u, other, j], recv_sem=self.sr.at[u, pair],
                device_id=(v, t), device_id_type=MESH,
            )

        def sum_wait(self, u, source, t):
            span = self.span(t)
            here = self.summed.at[u, source, :, span]
            pltpu.make_async_remote_copy(
                src_ref=here, dst_ref=here, send_sem=self.fs.at[u, source, 0], recv_sem=self.sr.at[u, source],
                device_id=(v, partner), device_id_type=MESH,
            ).wait_recv()

        def dir_copy(self, u, t):
            span = self.span(t)
            return pltpu.make_async_remote_copy(
                src_ref=self.wire.at[u, at_rows(t), span], dst_ref=self.direct.at[u, :, span],
                send_sem=self.ds.at[u], recv_sem=self.dr.at[u],
                device_id=(v, partner), device_id_type=MESH,
            )

        def product(self, u, left, right):
            got = jnp.dot(left[...], right, preferred_element_type=F32)
            self.part[u] = got
            self.wire[u] = got.astype(BF16)

        def send_relays(self, u):
            for k in range(1, pairs):
                @pl.when(outer(k))
                def _():
                    def send(other):
                        for j in range(2):
                            self.relay_copy(u, other, j).start()

                    self.by(lax.rem(pair + k, pairs), pairs, send)

        def send_sums(self, u):
            for k in range(1, pairs):
                @pl.when(jnp.logical_not(outer(k)))
                def _():
                    def send(other):
                        for j in range(2):
                            self.relay_copy(u, other, j).wait_recv()
                            own = self.part[u, at_rows(2 * other + j), :]
                            self.fwd[u, other, j] = (own + self.relay[u, other, j].astype(F32)).astype(BF16)
                            self.fwd_copy(u, other, j).start()

                    self.by(lax.rem(pair + k, pairs), pairs, send)

        def send_direct(self, u):
            self.by(partner, n, lambda t: self.dir_copy(u, t).start())

        def total(self, u):
            def wait(t):
                self.dir_copy(u, t).wait_recv()
                for k in range(1, pairs):
                    self.sum_wait(u, lax.rem(pair + k, pairs), t)

            self.by(s, n, wait)
            got = self.part[u, at_rows(s), :] + self.direct[u].astype(F32)
            for k in range(1, pairs):
                got = got + self.summed[u, lax.rem(pair + k, pairs)].astype(F32)
            return got

        def finish(self, units):
            for u in range(units):
                self.by(partner, n, lambda t: self.dir_copy(u, t).wait_send())
                for k in range(1, pairs):
                    def relays(other):
                        for j in range(2):
                            self.relay_copy(u, other, j).wait_send()

                    def sums(other):
                        for j in range(2):
                            self.fwd_copy(u, other, j).wait_send()

                    other = lax.rem(pair + k, pairs)

                    @pl.when(outer(k))
                    def _():
                        self.by(other, pairs, relays)

                    @pl.when(jnp.logical_not(outer(k)))
                    def _():
                        self.by(other, pairs, sums)

    own = Group(
        fold, own_part, own_wire, own_relay, own_fwd, own_summed, own_direct,
        own_rs, own_rr, own_fs, own_sr, own_ds, own_dr,
    )
    follow = Group(
        False, next_part, next_wire, next_relay, next_fwd, next_summed, next_direct,
        next_rs, next_rr, next_fs, next_sr, next_ds, next_dr,
    )

    def squares(values):
        values = values.astype(F32)
        return (values * values).astype(BF16)

    own.product(0, wt, d_ref[...])
    pl.semaphore_wait(barrier, 3 * n - 1)
    for h in range(2):
        shift(h).start()
    own.send_relays(0)
    sq[...] = squares(d_ref[...])
    own.product(1, qt, sq[...])
    own.send_relays(1)
    late = outer(1) if pairs > 1 else jnp.logical_and(odd == 0, odd == 1)

    for u in range(2):
        own.send_direct(u)
    for h in range(2):
        shift(h).wait_recv()
        follow.product(2 * h, wt, after[:, cols(h)])
        follow.send_relays(2 * h)
        sq[:, cols(h)] = squares(after[:, cols(h)])
        follow.product(2 * h + 1, qt, sq[:, cols(h)])
        follow.send_relays(2 * h + 1)

        @pl.when(jnp.logical_not(late))
        def _():
            for u in range(2 * h, 2 * h + 2):
                follow.send_direct(u)

        if h == 0:
            for u in range(2):
                own.send_sums(u)

    @pl.when(late)
    def _():
        for u in range(4):
            follow.send_direct(u)

    for u in range(4):
        follow.send_sums(u)

    def turn_copy(t, slot):
        return pltpu.make_async_remote_copy(
            src_ref=turned.at[t * rows:(t + 1) * rows], dst_ref=before.at[slot],
            send_sem=t_send.at[t], recv_sem=t_recv.at[slot],
            device_id=(nxt, t), device_id_type=MESH,
        )

    def mirror_copy(t, slot):
        return pltpu.make_async_remote_copy(
            src_ref=own_turned.at[t * rows:(t + 1) * rows], dst_ref=mirrored.at[slot],
            send_sem=m_send.at[t], recv_sem=m_recv.at[slot],
            device_id=(v, t), device_id_type=MESH,
        )

    for h in range(2):
        stat = follow.total(2 * h) / jnp.sqrt(follow.total(2 * h + 1) + 1e-05)
        out_ref[:, 2 * width + h * half:2 * width + (h + 1) * half] = stat
        turned[cols(h), :] = stat.T.astype(BF16)
        for t in range(h * pairs, (h + 1) * pairs):
            turn_copy(t, s).start()
    stat = own.total(0) / jnp.sqrt(own.total(1) + 1e-05)
    if fold:
        own_turned[...] = stat.T.astype(BF16)
        for t in range(n):
            @pl.when(owns(s, t))
            def _():
                mirror_copy(t, s).start()
    out_ref[:, width:2 * width] = stat
    for t in range(n):
        turn_copy(t, t).wait_recv()
        out_ref[:, t * rows:(t + 1) * rows] = before[t].astype(F32)
    if fold:
        for t in range(n):
            @pl.when(owns(t, s))
            def _():
                mirror_copy(t, t).wait_recv()
                out_ref[:, width + t * rows:width + (t + 1) * rows] = mirrored[t].astype(F32)

            @pl.when(owns(s, t))
            def _():
                mirror_copy(t, t).wait_send()

    for h in range(2):
        shift(h).wait_send()
    own.finish(2)
    follow.finish(4)
    for t in range(n):
        turn_copy(t, t).wait_send()


REDUCER = (0, 0, 0, 3, 1, 2, 3, 2, 3, 3, 0, 0, 2, 3, 0, 1, 1, 3, 0, 2, 2, 3, 3, 3, 3, 3)
PLAN = (
    (3, 6, 8, 9, 5, 7, 4, -1, 22, 13, 17, 21, 25, -2, 23, 24, 19, 12, 20, 15, 16, 0, 1, 2, 10, 14, 18, 11),
    (3, 6, 8, 9, 5, 7, 4, -1, 22, 13, 17, 21, 25, -2, 23, 24, 19, 12, 20, 15, 16, 0, 1, 2, 10, 14, 18, 11),
    (3, 6, 8, 9, 5, 7, 0, -1, 22, 13, 1, 17, 2, 21, 4, 25, -2, 23, 10, 24, 14, 18, 19, 11, 12, 20, 15, 16),
    (3, 6, 8, 9, 5, 7, 0, 1, 2, 4, -1, 22, 13, 17, 21, 25, 10, -2, 23, 24, 14, 19, 12, 18, 20, 11, 15, 16),
    (0, 1, 3, 2, 4, 6, 8, 9, -1, 10, 5, 14, 7, 18, 22, -2, 11, 13, 15, 17, 16, 21, 25, 23, 24, 19, 12, 20),
    (0, 3, 1, 6, 2, 8, 4, 9, 5, 7, -1, 10, 22, 13, 14, 18, 17, 21, -2, 11, 25, 15, 23, 16, 24, 19, 12, 20),
    (0, 1, 2, 4, 5, 7, -1, 10, 14, 18, -2, 11, 15, 16, 19, 12, 20, 3, 6, 8, 9, 22, 13, 17, 21, 25, 23, 24),
    (0, 1, 2, 4, 5, 7, -1, 10, 14, 18, -2, 11, 15, 16, 19, 12, 20, 3, 6, 8, 9, 22, 13, 17, 21, 25, 23, 24),
)


def line_kernel(
    nv, n, dosage_ref, class_hbm, effect_hbm, out_ref,
    d_ref, class_ref, effect_ref, after, wt, qt, sq, sq_after, dt, w_after, trait_column, parts,
    wire, near, joined, far, d_wire, d_near, d_joined, d_far, stat_out, stat_in,
    open_sem, load_sem, d_send, d_recv, near_send, near_recv, far_send, far_recv, stat_send, stat_recv,
):
    depth, width = d_ref.shape
    rows, half = width // n, width // 2
    v, s = lax.axis_index("var"), lax.axis_index("smp")
    nxt, prv = lax.rem(v + 1, nv), lax.rem(v + nv - 1, nv)

    loads = [
        pltpu.make_async_copy(dosage_ref, d_ref, load_sem.at[0]),
        pltpu.make_async_copy(class_hbm, class_ref, load_sem.at[1]),
        pltpu.make_async_copy(effect_hbm, effect_ref, load_sem.at[2]),
    ]
    for load in loads:
        load.start()
    barrier = pltpu.get_barrier_semaphore()
    host = n - 1

    def greet(target):
        pl.semaphore_signal(barrier, inc=1, device_id=target, device_id_type=MESH)

    greet((nxt, s))
    greet((prv, host))
    for role in range(n):
        @pl.when(s == role)
        def _():
            for other in {role - 1, role + 1, host} - {-1, n, role}:
                greet((v, other))

    for load in loads:
        load.wait()

    tiles = [(True, a, b) for a in range(n) for b in range(a, n)] + [(False, a, b) for a in range(n) for b in range(n)]
    order = {tile: at for at, tile in enumerate(tiles)}
    number = {tile: at for at, tile in enumerate(t for t in tiles if not diagonal(t))}
    spread = [b for h in range(n // 2) for b in (h, n - 1 - h)]

    def at_of(tile):
        return REDUCER[order[tile]]

    def block(index):
        return slice(index * rows, (index + 1) * rows)

    def cols(h):
        return slice(h * half, (h + 1) * half)

    def roles(body):
        for role in range(n):
            pl.when(s == role)(functools.partial(body, role))

    def plans(body):
        for at in range(2 * n):
            pl.when(2 * s + lax.rem(v, 2) == at)(functools.partial(body, at // 2, PLAN[at]))

    line = lax.broadcasted_iota(jnp.int32, (rows, rows), 0)
    column = lax.broadcasted_iota(jnp.int32, (rows, rows), 1)

    def slot(buffers, tile):
        plain, packed = buffers
        return packed.at[tile[1]] if diagonal(tile) else plain.at[number[tile]]

    def part(tile):
        same, a, b = tile
        first = 0 if same else 2
        b = b if same else spread.index(b)
        x, f = parts[first, block(a), block(b)], parts[first + 1, block(a), block(b)]
        if not diagonal(tile):
            return x, f
        middle = jnp.sum(jnp.where(line == column, f, 0.0), axis=0, keepdims=True)
        return jnp.where(line <= column, x, f), jnp.broadcast_to(middle, (EXTRA, rows))

    def places(tile):
        return (slice(0, rows), slice(rows, rows + EXTRA)) if diagonal(tile) else (0, 1)

    def put(buffers, tile, values):
        for where, value in zip(places(tile), values):
            slot(buffers, tile)[where] = value.astype(BF16)

    def get(buffers, tile):
        return [slot(buffers, tile)[where].astype(F32) for where in places(tile)]

    WIRE, NEAR, JOINED, FAR = (wire, d_wire), (near, d_near), (joined, d_joined), (far, d_far)

    def near_copy(tile, target):
        return pltpu.make_async_remote_copy(
            src_ref=slot(WIRE, tile), dst_ref=slot(NEAR, tile),
            send_sem=near_send.at[order[tile]], recv_sem=near_recv.at[order[tile]],
            device_id=(v, target), device_id_type=MESH,
        )

    def far_copy(tile, target):
        return pltpu.make_async_remote_copy(
            src_ref=slot(JOINED, tile), dst_ref=slot(FAR, tile),
            send_sem=far_send.at[order[tile]], recv_sem=far_recv.at[order[tile]],
            device_id=(v, target), device_id_type=MESH,
        )

    def stat_copy(tile, turned, target, to):
        return pltpu.make_async_remote_copy(
            src_ref=stat_out.at[order[tile], turned], dst_ref=stat_in.at[to],
            send_sem=stat_send.at[order[tile], turned], recv_sem=stat_recv.at[to],
            device_id=target, device_id_type=MESH,
        )

    def shift(at):
        return pltpu.make_async_remote_copy(
            src_ref=d_ref.at[:, block(spread[at])], dst_ref=after.at[:, block(at)],
            send_sem=d_send.at[at], recv_sem=d_recv.at[at],
            device_id=(prv, s), device_id_type=MESH,
        )

    def outer(role):
        return role in (0, n - 1)

    def kind(role, tile):
        target = at_of(tile)
        if target == role:
            return end
        if outer(role):
            return start
        return hand_on if target == role ^ 1 else join

    def mine(role, *acts):
        return [tile for tile in tiles if kind(role, tile) in acts]

    def start(role, tile):
        put(WIRE, tile, part(tile))
        near_copy(tile, role ^ 1).start()

    def join(role, tile):
        near_copy(tile, role ^ 1).wait_recv()
        put(JOINED, tile, [x + y for x, y in zip(part(tile), get(NEAR, tile))])
        far_copy(tile, n - 1 - role).start()

    def hand_on(role, tile):
        far_copy(tile, n - 1 - role).wait_recv()
        put(WIRE, tile, [x + y for x, y in zip(part(tile), get(FAR, tile))])
        near_copy(tile, role ^ 1).start()

    def goals(role, tile):
        same, a, b = tile
        if not same:
            return [(0, (v, a), a == role, 2 * n + b), (1, (nxt, b), False, a)]
        return [(0, (v, a), a == role, n + b)] + ([(1, (v, b), b == role, n + a)] if a != b else [])

    def end(role, tile):
        near_copy(tile, role ^ 1).wait_recv()
        x, f = [p + q for p, q in zip(part(tile), get(NEAR, tile))]
        if not outer(role):
            far_copy(tile, n - 1 - role).wait_recv()
            x, f = [p + q for p, q in zip((x, f), get(FAR, tile))]
        if diagonal(tile):
            packed, middle = x, f[:1]
            mirrored = packed.T
            x = jnp.where(line <= column, packed, mirrored)
            f = jnp.where(line == column, middle, jnp.where(line > column, packed, mirrored))
        stat = x / jnp.sqrt(f + 1e-05)
        for turned, target, local, to in goals(role, tile):
            value = stat.T if turned else stat
            if local:
                out_ref[:, block(to)] = value
            else:
                stat_out[order[tile], turned] = value.astype(BF16)
                stat_copy(tile, turned, target, to).start()

    classes = effect_ref.shape[0]
    mean = effect_ref[0]
    for c in range(1, classes):
        mean = mean + effect_ref[c]
    mean = mean / classes
    picked = class_ref[...]
    trait = jnp.zeros(picked.shape, F32)
    for c in range(classes):
        trait = jnp.where(picked == c, effect_ref[c] - mean, trait)
    for at in range(0, width, LANES):
        values = d_ref[:, at:at + LANES].astype(F32).T
        wt[at:at + LANES, :] = (values * trait).astype(BF16)
        qt[at:at + LANES, :] = (values * values).astype(BF16)
        dt[at:at + LANES, :] = values.astype(BF16)
    trait_column[...] = jnp.broadcast_to(trait, (LANES, depth)).T

    def squares(values):
        values = values.astype(F32)
        return (values * values).astype(BF16)

    sq[...] = squares(d_ref[...])
    for h in range(2):
        parts[0, cols(h), h * half:] = jnp.dot(wt[cols(h), :], d_ref[:, h * half:], preferred_element_type=F32)
        parts[1, cols(h), h * half:] = jnp.dot(qt[cols(h), :], sq[:, h * half:], preferred_element_type=F32)

    def enter(role):
        if role != host:
            pl.semaphore_wait(barrier, len({role - 1, role + 1} - {-1}) + 1)
        else:
            pl.semaphore_wait(barrier, 2 * n)
            for other in range(host):
                pl.semaphore_signal(open_sem, inc=1, device_id=(v, other), device_id_type=MESH)

    def run(stage):
        def body(role, plan):
            marks = [-1] + [plan.index(-1 - h) for h in range(2)] + [len(plan)]
            first_end = [at for at in plan if at >= 0 and kind(role, tiles[at]) is end][0]
            for at in plan[marks[stage] + 1:marks[stage + 1]]:
                if at == first_end and role != host:
                    pl.semaphore_wait(open_sem, 1)
                kind(role, tiles[at])(role, tiles[at])

        plans(body)

    def follow(h):
        for at in range(h * n // 2, (h + 1) * n // 2):
            shift(at).wait_recv()
        sq_after[:, cols(h)] = squares(after[:, cols(h)])
        for at in range(h * half, (h + 1) * half, LANES):
            w_after[:, at:at + LANES] = (after[:, at:at + LANES].astype(F32) * trait_column[...]).astype(BF16)
        cross = jnp.dot(wt[...], after[:, cols(h)], preferred_element_type=F32)
        cross = cross + jnp.dot(dt[...], w_after[:, cols(h)], preferred_element_type=F32)
        parts[2, :, cols(h)] = 0.5 * cross
        parts[3, :, cols(h)] = jnp.dot(qt[...], sq_after[:, cols(h)], preferred_element_type=F32)

    roles(enter)
    for at in range(n):
        shift(at).start()
    run(0)
    follow(0)
    run(1)
    follow(1)
    run(2)

    def close(role):
        for tile in tiles:
            for turned, target, local, to in goals(at_of(tile), tile):
                here = tile[2] if turned else tile[1]
                if here == role and not local:
                    arrived = pltpu.make_async_remote_copy(
                        src_ref=stat_in.at[to], dst_ref=stat_in.at[to],
                        send_sem=stat_send.at[0, 0], recv_sem=stat_recv.at[to],
                        device_id=(v, role ^ 1), device_id_type=MESH,
                    )
                    arrived.wait_recv()
                    out_ref[:, block(to)] = stat_in[to].astype(F32)
        for tile in mine(role, start, hand_on):
            near_copy(tile, role ^ 1).wait_send()
        for tile in mine(role, join):
            far_copy(tile, n - 1 - role).wait_send()
        for tile in mine(role, end):
            for turned, target, local, to in goals(role, tile):
                if not local:
                    stat_copy(tile, turned, target, to).wait_send()

    roles(close)
    for at in range(n):
        shift(at).wait_send()


def diagonal(tile):
    return tile[0] and tile[1] == tile[2]


def solution(mesh):
    nv, n = mesh.shape["var"], mesh.shape["smp"]

    def shards(dosage, trait_class, class_effect):
        depth, width = dosage.shape
        rows, half, pairs = width // n, width // 2, n // 2
        dma, vmem = pltpu.SemaphoreType.DMA, pltpu.VMEM

        def call(body, scratch):
            return pl.pallas_call(
                functools.partial(body, nv, n),
                out_shape=jax.ShapeDtypeStruct((rows, 3 * width), F32),
                in_specs=[pl.BlockSpec(memory_space=pltpu.HBM)] * 3,
                out_specs=pl.BlockSpec(memory_space=vmem),
                scratch_shapes=[
                    vmem((depth, width), BF16),
                    vmem((1, depth), jnp.int32),
                    pltpu.SMEM(class_effect.shape, F32),
                    vmem((depth, width), BF16),
                    vmem((width, depth), BF16),
                    vmem((width, depth), BF16),
                    vmem((depth, width), BF16),
                    *scratch,
                ],
                compiler_params=pltpu.CompilerParams(
                    collective_id=0, has_side_effects=True, vmem_limit_bytes=32 * 1024 * 1024
                ),
            )(*(pltpu.with_memory_space_constraint(x, pltpu.HBM) for x in (dosage, trait_class.reshape(1, depth), class_effect)))

        if n == 4 and rows % LANES == 0:
            tiles = n * (n + 1) // 2 + n * n
            return call(line_kernel, [
                vmem((depth, width), BF16),
                vmem((width, depth), BF16),
                vmem((depth, width), BF16),
                vmem((depth, LANES), F32),
                vmem((4, width, width), F32),
                *[vmem((tiles - n, 2, rows, rows), BF16)] * 4,
                *[vmem((n, rows + EXTRA, rows), BF16)] * 4,
                vmem((tiles, 2, rows, rows), BF16),
                vmem((3 * n, rows, rows), BF16),
                pltpu.SemaphoreType.REGULAR,
                dma((3,)), dma((n,)), dma((n,)),
                *[dma((tiles,))] * 4,
                dma((tiles, 2)), dma((3 * n,)),
            ])

        def buffers(units, wide):
            return [
                vmem((units, width, wide), F32),
                vmem((units, width, wide), BF16),
                vmem((units, pairs, 2, rows, wide), BF16),
                vmem((units, pairs, 2, rows, wide), BF16),
                vmem((units, pairs, rows, wide), BF16),
                vmem((units, rows, wide), BF16),
            ]

        def semaphores(units):
            return [
                dma((units, pairs, 2)), dma((units, pairs, 2)), dma((units, pairs, 2)),
                dma((units, pairs)), dma((units,)), dma((units,)),
            ]

        return call(kernel, [
            vmem((width, rows), BF16),
            vmem((n, rows, rows), BF16),
            vmem((width, rows), BF16),
            vmem((n, rows, rows), BF16),
            *buffers(2, width),
            *buffers(4, half),
            dma((3,)), dma((2,)), dma((2,)),
            dma((n,)), dma((n,)), dma((n,)), dma((n,)),
            *semaphores(2),
            *semaphores(4),
        ])

    in_specs = (P("smp", "var"), P("smp"), P())
    out_specs = P(("var", "smp"), None)
    return jax.shard_map(shards, mesh=mesh, in_specs=in_specs, out_specs=out_specs, check_vma=False)
```

```python
import functools

import jax
import jax.numpy as jnp
from jax import lax
from jax.experimental import pallas as pl
from jax.experimental.pallas import tpu as pltpu
from jax.sharding import PartitionSpec as P

MESH = pl.DeviceIdType.MESH
F32, BF16 = jnp.float32, jnp.bfloat16
LANES = 128
EXTRA = 16


def kernel(
    nv, n, dosage_ref, class_hbm, effect_hbm, out_ref,
    d_ref, class_ref, effect_ref, after, wt, qt, sq, turned, before, own_turned, mirrored,
    own_part, own_wire, own_relay, own_fwd, own_summed, own_direct,
    next_part, next_wire, next_relay, next_fwd, next_summed, next_direct,
    load_sem, d_send, d_recv, t_send, t_recv, m_send, m_recv,
    own_rs, own_rr, own_fs, own_sr, own_ds, own_dr,
    next_rs, next_rr, next_fs, next_sr, next_ds, next_dr,
):
    depth, width = d_ref.shape
    rows, half, pairs = width // n, width // 2, n // 2
    fold = rows % LANES == 0
    v, s = lax.axis_index("var"), lax.axis_index("smp")
    nxt, prv = lax.rem(v + 1, nv), lax.rem(v + nv - 1, nv)
    pair, odd = s // 2, lax.rem(s, 2)
    partner = s + 1 - 2 * odd

    loads = [
        pltpu.make_async_copy(dosage_ref, d_ref, load_sem.at[0]),
        pltpu.make_async_copy(class_hbm, class_ref, load_sem.at[1]),
        pltpu.make_async_copy(effect_hbm, effect_ref, load_sem.at[2]),
    ]
    for load in loads:
        load.start()
    barrier = pltpu.get_barrier_semaphore()
    for near in (nxt, prv):
        for step in range(n):
            pl.semaphore_signal(barrier, inc=1, device_id=(near, lax.rem(s + step, n)), device_id_type=MESH)
    for step in range(1, n):
        pl.semaphore_signal(barrier, inc=1, device_id=(v, lax.rem(s + step, n)), device_id_type=MESH)
    for load in loads:
        load.wait()

    def cols(h):
        return slice(h * half, (h + 1) * half)

    def shift(h):
        return pltpu.make_async_remote_copy(
            src_ref=d_ref.at[:, cols(h)], dst_ref=after.at[:, cols(h)],
            send_sem=d_send.at[h], recv_sem=d_recv.at[h],
            device_id=(prv, s), device_id_type=MESH,
        )

    classes = effect_ref.shape[0]
    mean = effect_ref[0]
    for c in range(1, classes):
        mean = mean + effect_ref[c]
    mean = mean / classes
    picked = class_ref[...]
    trait = jnp.zeros(picked.shape, F32)
    for c in range(classes):
        trait = jnp.where(picked == c, effect_ref[c] - mean, trait)
    for at in range(0, width, LANES):
        values = d_ref[:, at:at + LANES].astype(F32).T
        wt[at:at + LANES, :] = (values * trait).astype(BF16)
        qt[at:at + LANES, :] = (values * values).astype(BF16)

    def owns(a, c):
        from_a, from_c = abs_of(2 * a - (n - 1)), abs_of(2 * c - (n - 1))
        return jnp.logical_or(from_a > from_c, jnp.logical_and(from_a == from_c, a < c))

    def abs_of(x):
        return lax.max(x, -x) if isinstance(x, jax.Array) else jnp.int32(abs(x))

    def extent(t):
        if not fold:
            return slice(0, width)
        first, last = (t, n - 1 - t) if t < pairs else (n - t, t)
        return slice(first * rows, (last + 1) * rows)

    def cases(index, count, body):
        for known in range(count):
            pl.when(index == known)(functools.partial(body, known))

    def at_rows(index):
        return pl.ds(pl.multiple_of(index * rows, rows), rows)

    def outer(k):
        higher = lax.rem(pair + k, pairs) > pair
        return jnp.logical_or(
            jnp.logical_and(higher, odd == 0), jnp.logical_and(jnp.logical_not(higher), odd == 1)
        )

    class Group:
        def __init__(self, folded, part, wire, relay, fwd, summed, direct, rs, rr, fs, sr, ds, dr):
            self.folded, self.part, self.wire, self.relay = folded, part, wire, relay
            self.fwd, self.summed, self.direct = fwd, summed, direct
            self.rs, self.rr, self.fs, self.sr, self.ds, self.dr = rs, rr, fs, sr, ds, dr

        def span(self, t):
            return extent(t) if self.folded else slice(None)

        def by(self, index, count, body):
            if self.folded:
                cases(index, count, body)
            else:
                body(index)

        def relay_copy(self, u, other, j):
            t = 2 * other + j
            span = self.span(t)
            return pltpu.make_async_remote_copy(
                src_ref=self.wire.at[u, at_rows(t), span], dst_ref=self.relay.at[u, other, j, :, span],
                send_sem=self.rs.at[u, other, j], recv_sem=self.rr.at[u, other, j],
                device_id=(v, partner), device_id_type=MESH,
            )

        def fwd_copy(self, u, other, j):
            t = 2 * other + j
            span = self.span(t)
            return pltpu.make_async_remote_copy(
                src_ref=self.fwd.at[u, other, j, :, span], dst_ref=self.summed.at[u, pair, :, span],
                send_sem=self.fs.at[u, other, j], recv_sem=self.sr.at[u, pair],
                device_id=(v, t), device_id_type=MESH,
            )

        def sum_wait(self, u, source, t):
            span = self.span(t)
            here = self.summed.at[u, source, :, span]
            pltpu.make_async_remote_copy(
                src_ref=here, dst_ref=here, send_sem=self.fs.at[u, source, 0], recv_sem=self.sr.at[u, source],
                device_id=(v, partner), device_id_type=MESH,
            ).wait_recv()

        def dir_copy(self, u, t):
            span = self.span(t)
            return pltpu.make_async_remote_copy(
                src_ref=self.wire.at[u, at_rows(t), span], dst_ref=self.direct.at[u, :, span],
                send_sem=self.ds.at[u], recv_sem=self.dr.at[u],
                device_id=(v, partner), device_id_type=MESH,
            )

        def product(self, u, left, right):
            got = jnp.dot(left[...], right, preferred_element_type=F32)
            self.part[u] = got
            self.wire[u] = got.astype(BF16)

        def send_relays(self, u):
            for k in range(1, pairs):
                @pl.when(outer(k))
                def _():
                    def send(other):
                        for j in range(2):
                            self.relay_copy(u, other, j).start()

                    self.by(lax.rem(pair + k, pairs), pairs, send)

        def send_sums(self, u):
            for k in range(1, pairs):
                @pl.when(jnp.logical_not(outer(k)))
                def _():
                    def send(other):
                        for j in range(2):
                            self.relay_copy(u, other, j).wait_recv()
                            own = self.part[u, at_rows(2 * other + j), :]
                            self.fwd[u, other, j] = (own + self.relay[u, other, j].astype(F32)).astype(BF16)
                            self.fwd_copy(u, other, j).start()

                    self.by(lax.rem(pair + k, pairs), pairs, send)

        def send_direct(self, u):
            self.by(partner, n, lambda t: self.dir_copy(u, t).start())

        def total(self, u):
            def wait(t):
                self.dir_copy(u, t).wait_recv()
                for k in range(1, pairs):
                    self.sum_wait(u, lax.rem(pair + k, pairs), t)

            self.by(s, n, wait)
            got = self.part[u, at_rows(s), :] + self.direct[u].astype(F32)
            for k in range(1, pairs):
                got = got + self.summed[u, lax.rem(pair + k, pairs)].astype(F32)
            return got

        def finish(self, units):
            for u in range(units):
                self.by(partner, n, lambda t: self.dir_copy(u, t).wait_send())
                for k in range(1, pairs):
                    def relays(other):
                        for j in range(2):
                            self.relay_copy(u, other, j).wait_send()

                    def sums(other):
                        for j in range(2):
                            self.fwd_copy(u, other, j).wait_send()

                    other = lax.rem(pair + k, pairs)

                    @pl.when(outer(k))
                    def _():
                        self.by(other, pairs, relays)

                    @pl.when(jnp.logical_not(outer(k)))
                    def _():
                        self.by(other, pairs, sums)

    own = Group(
        fold, own_part, own_wire, own_relay, own_fwd, own_summed, own_direct,
        own_rs, own_rr, own_fs, own_sr, own_ds, own_dr,
    )
    follow = Group(
        False, next_part, next_wire, next_relay, next_fwd, next_summed, next_direct,
        next_rs, next_rr, next_fs, next_sr, next_ds, next_dr,
    )

    def squares(values):
        values = values.astype(F32)
        return (values * values).astype(BF16)

    own.product(0, wt, d_ref[...])
    pl.semaphore_wait(barrier, 3 * n - 1)
    for h in range(2):
        shift(h).start()
    own.send_relays(0)
    sq[...] = squares(d_ref[...])
    own.product(1, qt, sq[...])
    own.send_relays(1)
    late = outer(1) if pairs > 1 else jnp.logical_and(odd == 0, odd == 1)

    for u in range(2):
        own.send_direct(u)
    for h in range(2):
        shift(h).wait_recv()
        follow.product(2 * h, wt, after[:, cols(h)])
        follow.send_relays(2 * h)
        sq[:, cols(h)] = squares(after[:, cols(h)])
        follow.product(2 * h + 1, qt, sq[:, cols(h)])
        follow.send_relays(2 * h + 1)

        @pl.when(jnp.logical_not(late))
        def _():
            for u in range(2 * h, 2 * h + 2):
                follow.send_direct(u)

        if h == 0:
            for u in range(2):
                own.send_sums(u)

    @pl.when(late)
    def _():
        for u in range(4):
            follow.send_direct(u)

    for u in range(4):
        follow.send_sums(u)

    def turn_copy(t, slot):
        return pltpu.make_async_remote_copy(
            src_ref=turned.at[t * rows:(t + 1) * rows], dst_ref=before.at[slot],
            send_sem=t_send.at[t], recv_sem=t_recv.at[slot],
            device_id=(nxt, t), device_id_type=MESH,
        )

    def mirror_copy(t, slot):
        return pltpu.make_async_remote_copy(
            src_ref=own_turned.at[t * rows:(t + 1) * rows], dst_ref=mirrored.at[slot],
            send_sem=m_send.at[t], recv_sem=m_recv.at[slot],
            device_id=(v, t), device_id_type=MESH,
        )

    for h in range(2):
        stat = follow.total(2 * h) / jnp.sqrt(follow.total(2 * h + 1) + 1e-05)
        out_ref[:, 2 * width + h * half:2 * width + (h + 1) * half] = stat
        turned[cols(h), :] = stat.T.astype(BF16)
        for t in range(h * pairs, (h + 1) * pairs):
            turn_copy(t, s).start()
    stat = own.total(0) / jnp.sqrt(own.total(1) + 1e-05)
    if fold:
        own_turned[...] = stat.T.astype(BF16)
        for t in range(n):
            @pl.when(owns(s, t))
            def _():
                mirror_copy(t, s).start()
    out_ref[:, width:2 * width] = stat
    for t in range(n):
        turn_copy(t, t).wait_recv()
        out_ref[:, t * rows:(t + 1) * rows] = before[t].astype(F32)
    if fold:
        for t in range(n):
            @pl.when(owns(t, s))
            def _():
                mirror_copy(t, t).wait_recv()
                out_ref[:, width + t * rows:width + (t + 1) * rows] = mirrored[t].astype(F32)

            @pl.when(owns(s, t))
            def _():
                mirror_copy(t, t).wait_send()

    for h in range(2):
        shift(h).wait_send()
    own.finish(2)
    follow.finish(4)
    for t in range(n):
        turn_copy(t, t).wait_send()


REDUCER = (0, 0, 0, 3, 1, 2, 3, 2, 3, 3, 0, 0, 2, 3, 0, 1, 1, 3, 0, 2, 2, 3, 3, 3, 3, 3)
PLAN = (
    (3, 6, 8, 9, 5, 7, 4, -1, 22, 13, 17, 21, 25, -2, 23, 24, 19, 12, 20, 15, 16, 0, 1, 2, 10, 14, 18, 11),
    (3, 6, 8, 9, 5, 7, 4, -1, 22, 13, 17, 21, 25, -2, 23, 24, 19, 12, 20, 15, 16, 0, 1, 2, 10, 14, 18, 11),
    (3, 6, 8, 9, 5, 7, 0, -1, 22, 13, 1, 17, 2, 21, 4, 25, -2, 23, 10, 24, 14, 18, 19, 11, 12, 20, 15, 16),
    (3, 6, 8, 9, 5, 7, 0, 1, 2, 4, -1, 22, 13, 17, 21, 25, 10, -2, 23, 24, 14, 19, 18, 12, 11, 20, 15, 16),
    (0, 1, 3, 2, 4, 6, 8, 9, -1, 10, 5, 14, 7, 18, 22, -2, 11, 13, 15, 17, 16, 21, 25, 23, 24, 19, 12, 20),
    (0, 3, 1, 6, 2, 8, 4, 9, 5, 7, -1, 10, 22, 13, 14, 18, 17, 21, -2, 11, 25, 15, 23, 16, 24, 19, 12, 20),
    (0, 1, 2, 4, 5, 7, -1, 10, 14, 18, -2, 11, 15, 16, 19, 12, 20, 3, 6, 8, 9, 22, 13, 17, 21, 25, 23, 24),
    (0, 1, 2, 4, 5, 7, -1, 10, 14, 18, -2, 11, 15, 16, 19, 12, 20, 3, 6, 8, 9, 22, 13, 17, 21, 25, 23, 24),
)


def line_kernel(
    nv, n, dosage_ref, class_hbm, effect_hbm, out_ref,
    d_ref, class_ref, effect_ref, after, wt, qt, sq, sq_after, dt, w_after, trait_column, parts,
    wire, near, joined, far, d_wire, d_near, d_joined, d_far, stat_out, stat_in,
    open_sem, load_sem, d_send, d_recv, near_send, near_recv, far_send, far_recv, stat_send, stat_recv,
):
    depth, width = d_ref.shape
    rows, half = width // n, width // 2
    v, s = lax.axis_index("var"), lax.axis_index("smp")
    nxt, prv = lax.rem(v + 1, nv), lax.rem(v + nv - 1, nv)

    loads = [
        pltpu.make_async_copy(dosage_ref, d_ref, load_sem.at[0]),
        pltpu.make_async_copy(class_hbm, class_ref, load_sem.at[1]),
        pltpu.make_async_copy(effect_hbm, effect_ref, load_sem.at[2]),
    ]
    for load in loads:
        load.start()
    barrier = pltpu.get_barrier_semaphore()
    host = n - 1

    def greet(target):
        pl.semaphore_signal(barrier, inc=1, device_id=target, device_id_type=MESH)

    greet((nxt, s))
    greet((prv, host))
    for role in range(n):
        @pl.when(s == role)
        def _():
            for other in {role - 1, role + 1, host} - {-1, n, role}:
                greet((v, other))

    for load in loads:
        load.wait()

    tiles = [(True, a, b) for a in range(n) for b in range(a, n)] + [(False, a, b) for a in range(n) for b in range(n)]
    order = {tile: at for at, tile in enumerate(tiles)}
    number = {tile: at for at, tile in enumerate(t for t in tiles if not diagonal(t))}
    spread = [b for h in range(n // 2) for b in (h, n - 1 - h)]

    def at_of(tile):
        return REDUCER[order[tile]]

    def block(index):
        return slice(index * rows, (index + 1) * rows)

    def cols(h):
        return slice(h * half, (h + 1) * half)

    def roles(body):
        for role in range(n):
            pl.when(s == role)(functools.partial(body, role))

    def plans(body):
        for at in range(2 * n):
            pl.when(2 * s + lax.rem(v, 2) == at)(functools.partial(body, at // 2, PLAN[at]))

    line = lax.broadcasted_iota(jnp.int32, (rows, rows), 0)
    column = lax.broadcasted_iota(jnp.int32, (rows, rows), 1)

    def slot(buffers, tile):
        plain, packed = buffers
        return packed.at[tile[1]] if diagonal(tile) else plain.at[number[tile]]

    def part(tile):
        same, a, b = tile
        first = 0 if same else 2
        b = b if same else spread.index(b)
        x, f = parts[first, block(a), block(b)], parts[first + 1, block(a), block(b)]
        if not diagonal(tile):
            return x, f
        middle = jnp.sum(jnp.where(line == column, f, 0.0), axis=0, keepdims=True)
        return jnp.where(line <= column, x, f), jnp.broadcast_to(middle, (EXTRA, rows))

    def places(tile):
        return (slice(0, rows), slice(rows, rows + EXTRA)) if diagonal(tile) else (0, 1)

    def put(buffers, tile, values):
        for where, value in zip(places(tile), values):
            slot(buffers, tile)[where] = value.astype(BF16)

    def get(buffers, tile):
        return [slot(buffers, tile)[where].astype(F32) for where in places(tile)]

    WIRE, NEAR, JOINED, FAR = (wire, d_wire), (near, d_near), (joined, d_joined), (far, d_far)

    def near_copy(tile, target):
        return pltpu.make_async_remote_copy(
            src_ref=slot(WIRE, tile), dst_ref=slot(NEAR, tile),
            send_sem=near_send.at[order[tile]], recv_sem=near_recv.at[order[tile]],
            device_id=(v, target), device_id_type=MESH,
        )

    def far_copy(tile, target):
        return pltpu.make_async_remote_copy(
            src_ref=slot(JOINED, tile), dst_ref=slot(FAR, tile),
            send_sem=far_send.at[order[tile]], recv_sem=far_recv.at[order[tile]],
            device_id=(v, target), device_id_type=MESH,
        )

    def stat_copy(tile, turned, target, to):
        return pltpu.make_async_remote_copy(
            src_ref=stat_out.at[order[tile], turned], dst_ref=stat_in.at[to],
            send_sem=stat_send.at[order[tile], turned], recv_sem=stat_recv.at[to],
            device_id=target, device_id_type=MESH,
        )

    def shift(at):
        return pltpu.make_async_remote_copy(
            src_ref=d_ref.at[:, block(spread[at])], dst_ref=after.at[:, block(at)],
            send_sem=d_send.at[at], recv_sem=d_recv.at[at],
            device_id=(prv, s), device_id_type=MESH,
        )

    def outer(role):
        return role in (0, n - 1)

    def kind(role, tile):
        target = at_of(tile)
        if target == role:
            return end
        if outer(role):
            return start
        return hand_on if target == role ^ 1 else join

    def mine(role, *acts):
        return [tile for tile in tiles if kind(role, tile) in acts]

    def start(role, tile):
        put(WIRE, tile, part(tile))
        near_copy(tile, role ^ 1).start()

    def join(role, tile):
        near_copy(tile, role ^ 1).wait_recv()
        put(JOINED, tile, [x + y for x, y in zip(part(tile), get(NEAR, tile))])
        far_copy(tile, n - 1 - role).start()

    def hand_on(role, tile):
        far_copy(tile, n - 1 - role).wait_recv()
        put(WIRE, tile, [x + y for x, y in zip(part(tile), get(FAR, tile))])
        near_copy(tile, role ^ 1).start()

    def goals(role, tile):
        same, a, b = tile
        if not same:
            return [(0, (v, a), a == role, 2 * n + b), (1, (nxt, b), False, a)]
        return [(0, (v, a), a == role, n + b)] + ([(1, (v, b), b == role, n + a)] if a != b else [])

    def end(role, tile):
        near_copy(tile, role ^ 1).wait_recv()
        x, f = [p + q for p, q in zip(part(tile), get(NEAR, tile))]
        if not outer(role):
            far_copy(tile, n - 1 - role).wait_recv()
            x, f = [p + q for p, q in zip((x, f), get(FAR, tile))]
        if diagonal(tile):
            packed, middle = x, f[:1]
            mirrored = packed.T
            x = jnp.where(line <= column, packed, mirrored)
            f = jnp.where(line == column, middle, jnp.where(line > column, packed, mirrored))
        stat = x / jnp.sqrt(f + 1e-05)
        for turned, target, local, to in goals(role, tile):
            value = stat.T if turned else stat
            if local:
                out_ref[:, block(to)] = value
            else:
                stat_out[order[tile], turned] = value.astype(BF16)
                stat_copy(tile, turned, target, to).start()

    classes = effect_ref.shape[0]
    mean = effect_ref[0]
    for c in range(1, classes):
        mean = mean + effect_ref[c]
    mean = mean / classes
    picked = class_ref[...]
    trait = jnp.zeros(picked.shape, F32)
    for c in range(classes):
        trait = jnp.where(picked == c, effect_ref[c] - mean, trait)
    for at in range(0, width, LANES):
        values = d_ref[:, at:at + LANES].astype(F32).T
        wt[at:at + LANES, :] = (values * trait).astype(BF16)
        qt[at:at + LANES, :] = (values * values).astype(BF16)
        dt[at:at + LANES, :] = values.astype(BF16)
    trait_column[...] = jnp.broadcast_to(trait, (LANES, depth)).T

    def squares(values):
        values = values.astype(F32)
        return (values * values).astype(BF16)

    sq[...] = squares(d_ref[...])
    for h in range(2):
        parts[0, cols(h), h * half:] = jnp.dot(wt[cols(h), :], d_ref[:, h * half:], preferred_element_type=F32)
        parts[1, cols(h), h * half:] = jnp.dot(qt[cols(h), :], sq[:, h * half:], preferred_element_type=F32)

    def enter(role):
        if role != host:
            pl.semaphore_wait(barrier, len({role - 1, role + 1} - {-1}) + 1)
        else:
            pl.semaphore_wait(barrier, 2 * n)
            for other in range(host):
                pl.semaphore_signal(open_sem, inc=1, device_id=(v, other), device_id_type=MESH)

    def run(stage, which=None):
        def body(role, plan):
            if which is not None and outer(role) != which:
                return
            marks = [-1] + [plan.index(-1 - h) for h in range(2)] + [len(plan)]
            first_end = [at for at in plan if at >= 0 and kind(role, tiles[at]) is end][0]
            for at in plan[marks[stage] + 1:marks[stage + 1]]:
                if at == first_end and role != host:
                    pl.semaphore_wait(open_sem, 1)
                kind(role, tiles[at])(role, tiles[at])

        plans(body)

    def follow(h):
        for at in range(h * n // 2, (h + 1) * n // 2):
            shift(at).wait_recv()
        sq_after[:, cols(h)] = squares(after[:, cols(h)])
        for at in range(h * half, (h + 1) * half, LANES):
            w_after[:, at:at + LANES] = (after[:, at:at + LANES].astype(F32) * trait_column[...]).astype(BF16)
        cross = jnp.dot(wt[...], after[:, cols(h)], preferred_element_type=F32)
        cross = cross + jnp.dot(dt[...], w_after[:, cols(h)], preferred_element_type=F32)
        parts[2, :, cols(h)] = 0.5 * cross
        parts[3, :, cols(h)] = jnp.dot(qt[...], sq_after[:, cols(h)], preferred_element_type=F32)

    roles(enter)
    run(0, True)
    for at in range(n):
        shift(at).start()
    run(0, False)
    follow(0)
    run(1)
    follow(1)
    run(2)

    def close(role):
        for tile in tiles:
            for turned, target, local, to in goals(at_of(tile), tile):
                here = tile[2] if turned else tile[1]
                if here == role and not local:
                    arrived = pltpu.make_async_remote_copy(
                        src_ref=stat_in.at[to], dst_ref=stat_in.at[to],
                        send_sem=stat_send.at[0, 0], recv_sem=stat_recv.at[to],
                        device_id=(v, role ^ 1), device_id_type=MESH,
                    )
                    arrived.wait_recv()
                    out_ref[:, block(to)] = stat_in[to].astype(F32)
        for tile in mine(role, start, hand_on):
            near_copy(tile, role ^ 1).wait_send()
        for tile in mine(role, join):
            far_copy(tile, n - 1 - role).wait_send()
        for tile in mine(role, end):
            for turned, target, local, to in goals(role, tile):
                if not local:
                    stat_copy(tile, turned, target, to).wait_send()

    roles(close)
    for at in range(n):
        shift(at).wait_send()


def diagonal(tile):
    return tile[0] and tile[1] == tile[2]


def solution(mesh):
    nv, n = mesh.shape["var"], mesh.shape["smp"]

    def shards(dosage, trait_class, class_effect):
        depth, width = dosage.shape
        rows, half, pairs = width // n, width // 2, n // 2
        dma, vmem = pltpu.SemaphoreType.DMA, pltpu.VMEM

        def call(body, scratch):
            return pl.pallas_call(
                functools.partial(body, nv, n),
                out_shape=jax.ShapeDtypeStruct((rows, 3 * width), F32),
                in_specs=[pl.BlockSpec(memory_space=pltpu.HBM)] * 3,
                out_specs=pl.BlockSpec(memory_space=vmem),
                scratch_shapes=[
                    vmem((depth, width), BF16),
                    vmem((1, depth), jnp.int32),
                    pltpu.SMEM(class_effect.shape, F32),
                    vmem((depth, width), BF16),
                    vmem((width, depth), BF16),
                    vmem((width, depth), BF16),
                    vmem((depth, width), BF16),
                    *scratch,
                ],
                compiler_params=pltpu.CompilerParams(
                    collective_id=0, has_side_effects=True, vmem_limit_bytes=32 * 1024 * 1024
                ),
            )(*(pltpu.with_memory_space_constraint(x, pltpu.HBM) for x in (dosage, trait_class.reshape(1, depth), class_effect)))

        if n == 4 and rows % LANES == 0:
            tiles = n * (n + 1) // 2 + n * n
            return call(line_kernel, [
                vmem((depth, width), BF16),
                vmem((width, depth), BF16),
                vmem((depth, width), BF16),
                vmem((depth, LANES), F32),
                vmem((4, width, width), F32),
                *[vmem((tiles - n, 2, rows, rows), BF16)] * 4,
                *[vmem((n, rows + EXTRA, rows), BF16)] * 4,
                vmem((tiles, 2, rows, rows), BF16),
                vmem((3 * n, rows, rows), BF16),
                pltpu.SemaphoreType.REGULAR,
                dma((3,)), dma((n,)), dma((n,)),
                *[dma((tiles,))] * 4,
                dma((tiles, 2)), dma((3 * n,)),
            ])

        def buffers(units, wide):
            return [
                vmem((units, width, wide), F32),
                vmem((units, width, wide), BF16),
                vmem((units, pairs, 2, rows, wide), BF16),
                vmem((units, pairs, 2, rows, wide), BF16),
                vmem((units, pairs, rows, wide), BF16),
                vmem((units, rows, wide), BF16),
            ]

        def semaphores(units):
            return [
                dma((units, pairs, 2)), dma((units, pairs, 2)), dma((units, pairs, 2)),
                dma((units, pairs)), dma((units,)), dma((units,)),
            ]

        return call(kernel, [
            vmem((width, rows), BF16),
            vmem((n, rows, rows), BF16),
            vmem((width, rows), BF16),
            vmem((n, rows, rows), BF16),
            *buffers(2, width),
            *buffers(4, half),
            dma((3,)), dma((2,)), dma((2,)),
            dma((n,)), dma((n,)), dma((n,)), dma((n,)),
            *semaphores(2),
            *semaphores(4),
        ])

    in_specs = (P("smp", "var"), P("smp"), P())
    out_specs = P(("var", "smp"), None)
    return jax.shard_map(shards, mesh=mesh, in_specs=in_specs, out_specs=out_specs, check_vma=False)
```

```python
import functools

import jax
import jax.numpy as jnp
from jax import lax
from jax.experimental import pallas as pl
from jax.experimental.pallas import tpu as pltpu
from jax.sharding import PartitionSpec as P

MESH = pl.DeviceIdType.MESH
F32, BF16 = jnp.float32, jnp.bfloat16
LANES = 128
EXTRA = 16


def kernel(
    nv, n, dosage_ref, class_hbm, effect_hbm, out_ref,
    d_ref, class_ref, effect_ref, after, wt, qt, sq, turned, before, own_turned, mirrored,
    own_part, own_wire, own_relay, own_fwd, own_summed, own_direct,
    next_part, next_wire, next_relay, next_fwd, next_summed, next_direct,
    load_sem, d_send, d_recv, t_send, t_recv, m_send, m_recv,
    own_rs, own_rr, own_fs, own_sr, own_ds, own_dr,
    next_rs, next_rr, next_fs, next_sr, next_ds, next_dr,
):
    depth, width = d_ref.shape
    rows, half, pairs = width // n, width // 2, n // 2
    fold = rows % LANES == 0
    v, s = lax.axis_index("var"), lax.axis_index("smp")
    nxt, prv = lax.rem(v + 1, nv), lax.rem(v + nv - 1, nv)
    pair, odd = s // 2, lax.rem(s, 2)
    partner = s + 1 - 2 * odd

    loads = [
        pltpu.make_async_copy(dosage_ref, d_ref, load_sem.at[0]),
        pltpu.make_async_copy(class_hbm, class_ref, load_sem.at[1]),
        pltpu.make_async_copy(effect_hbm, effect_ref, load_sem.at[2]),
    ]
    for load in loads:
        load.start()
    barrier = pltpu.get_barrier_semaphore()
    for near in (nxt, prv):
        for step in range(n):
            pl.semaphore_signal(barrier, inc=1, device_id=(near, lax.rem(s + step, n)), device_id_type=MESH)
    for step in range(1, n):
        pl.semaphore_signal(barrier, inc=1, device_id=(v, lax.rem(s + step, n)), device_id_type=MESH)
    for load in loads:
        load.wait()

    def cols(h):
        return slice(h * half, (h + 1) * half)

    def shift(h):
        return pltpu.make_async_remote_copy(
            src_ref=d_ref.at[:, cols(h)], dst_ref=after.at[:, cols(h)],
            send_sem=d_send.at[h], recv_sem=d_recv.at[h],
            device_id=(prv, s), device_id_type=MESH,
        )

    classes = effect_ref.shape[0]
    mean = effect_ref[0]
    for c in range(1, classes):
        mean = mean + effect_ref[c]
    mean = mean / classes
    picked = class_ref[...]
    trait = jnp.zeros(picked.shape, F32)
    for c in range(classes):
        trait = jnp.where(picked == c, effect_ref[c] - mean, trait)
    for at in range(0, width, LANES):
        values = d_ref[:, at:at + LANES].astype(F32).T
        wt[at:at + LANES, :] = (values * trait).astype(BF16)
        qt[at:at + LANES, :] = (values * values).astype(BF16)

    def owns(a, c):
        from_a, from_c = abs_of(2 * a - (n - 1)), abs_of(2 * c - (n - 1))
        return jnp.logical_or(from_a > from_c, jnp.logical_and(from_a == from_c, a < c))

    def abs_of(x):
        return lax.max(x, -x) if isinstance(x, jax.Array) else jnp.int32(abs(x))

    def extent(t):
        if not fold:
            return slice(0, width)
        first, last = (t, n - 1 - t) if t < pairs else (n - t, t)
        return slice(first * rows, (last + 1) * rows)

    def cases(index, count, body):
        for known in range(count):
            pl.when(index == known)(functools.partial(body, known))

    def at_rows(index):
        return pl.ds(pl.multiple_of(index * rows, rows), rows)

    def outer(k):
        higher = lax.rem(pair + k, pairs) > pair
        return jnp.logical_or(
            jnp.logical_and(higher, odd == 0), jnp.logical_and(jnp.logical_not(higher), odd == 1)
        )

    class Group:
        def __init__(self, folded, part, wire, relay, fwd, summed, direct, rs, rr, fs, sr, ds, dr):
            self.folded, self.part, self.wire, self.relay = folded, part, wire, relay
            self.fwd, self.summed, self.direct = fwd, summed, direct
            self.rs, self.rr, self.fs, self.sr, self.ds, self.dr = rs, rr, fs, sr, ds, dr

        def span(self, t):
            return extent(t) if self.folded else slice(None)

        def by(self, index, count, body):
            if self.folded:
                cases(index, count, body)
            else:
                body(index)

        def relay_copy(self, u, other, j):
            t = 2 * other + j
            span = self.span(t)
            return pltpu.make_async_remote_copy(
                src_ref=self.wire.at[u, at_rows(t), span], dst_ref=self.relay.at[u, other, j, :, span],
                send_sem=self.rs.at[u, other, j], recv_sem=self.rr.at[u, other, j],
                device_id=(v, partner), device_id_type=MESH,
            )

        def fwd_copy(self, u, other, j):
            t = 2 * other + j
            span = self.span(t)
            return pltpu.make_async_remote_copy(
                src_ref=self.fwd.at[u, other, j, :, span], dst_ref=self.summed.at[u, pair, :, span],
                send_sem=self.fs.at[u, other, j], recv_sem=self.sr.at[u, pair],
                device_id=(v, t), device_id_type=MESH,
            )

        def sum_wait(self, u, source, t):
            span = self.span(t)
            here = self.summed.at[u, source, :, span]
            pltpu.make_async_remote_copy(
                src_ref=here, dst_ref=here, send_sem=self.fs.at[u, source, 0], recv_sem=self.sr.at[u, source],
                device_id=(v, partner), device_id_type=MESH,
            ).wait_recv()

        def dir_copy(self, u, t):
            span = self.span(t)
            return pltpu.make_async_remote_copy(
                src_ref=self.wire.at[u, at_rows(t), span], dst_ref=self.direct.at[u, :, span],
                send_sem=self.ds.at[u], recv_sem=self.dr.at[u],
                device_id=(v, partner), device_id_type=MESH,
            )

        def product(self, u, left, right):
            got = jnp.dot(left[...], right, preferred_element_type=F32)
            self.part[u] = got
            self.wire[u] = got.astype(BF16)

        def send_relays(self, u):
            for k in range(1, pairs):
                @pl.when(outer(k))
                def _():
                    def send(other):
                        for j in range(2):
                            self.relay_copy(u, other, j).start()

                    self.by(lax.rem(pair + k, pairs), pairs, send)

        def send_sums(self, u):
            for k in range(1, pairs):
                @pl.when(jnp.logical_not(outer(k)))
                def _():
                    def send(other):
                        for j in range(2):
                            self.relay_copy(u, other, j).wait_recv()
                            own = self.part[u, at_rows(2 * other + j), :]
                            self.fwd[u, other, j] = (own + self.relay[u, other, j].astype(F32)).astype(BF16)
                            self.fwd_copy(u, other, j).start()

                    self.by(lax.rem(pair + k, pairs), pairs, send)

        def send_direct(self, u):
            self.by(partner, n, lambda t: self.dir_copy(u, t).start())

        def total(self, u):
            def wait(t):
                self.dir_copy(u, t).wait_recv()
                for k in range(1, pairs):
                    self.sum_wait(u, lax.rem(pair + k, pairs), t)

            self.by(s, n, wait)
            got = self.part[u, at_rows(s), :] + self.direct[u].astype(F32)
            for k in range(1, pairs):
                got = got + self.summed[u, lax.rem(pair + k, pairs)].astype(F32)
            return got

        def finish(self, units):
            for u in range(units):
                self.by(partner, n, lambda t: self.dir_copy(u, t).wait_send())
                for k in range(1, pairs):
                    def relays(other):
                        for j in range(2):
                            self.relay_copy(u, other, j).wait_send()

                    def sums(other):
                        for j in range(2):
                            self.fwd_copy(u, other, j).wait_send()

                    other = lax.rem(pair + k, pairs)

                    @pl.when(outer(k))
                    def _():
                        self.by(other, pairs, relays)

                    @pl.when(jnp.logical_not(outer(k)))
                    def _():
                        self.by(other, pairs, sums)

    own = Group(
        fold, own_part, own_wire, own_relay, own_fwd, own_summed, own_direct,
        own_rs, own_rr, own_fs, own_sr, own_ds, own_dr,
    )
    follow = Group(
        False, next_part, next_wire, next_relay, next_fwd, next_summed, next_direct,
        next_rs, next_rr, next_fs, next_sr, next_ds, next_dr,
    )

    def squares(values):
        values = values.astype(F32)
        return (values * values).astype(BF16)

    own.product(0, wt, d_ref[...])
    pl.semaphore_wait(barrier, 3 * n - 1)
    for h in range(2):
        shift(h).start()
    own.send_relays(0)
    sq[...] = squares(d_ref[...])
    own.product(1, qt, sq[...])
    own.send_relays(1)
    late = outer(1) if pairs > 1 else jnp.logical_and(odd == 0, odd == 1)

    for u in range(2):
        own.send_direct(u)
    for h in range(2):
        shift(h).wait_recv()
        follow.product(2 * h, wt, after[:, cols(h)])
        follow.send_relays(2 * h)
        sq[:, cols(h)] = squares(after[:, cols(h)])
        follow.product(2 * h + 1, qt, sq[:, cols(h)])
        follow.send_relays(2 * h + 1)

        @pl.when(jnp.logical_not(late))
        def _():
            for u in range(2 * h, 2 * h + 2):
                follow.send_direct(u)

        if h == 0:
            for u in range(2):
                own.send_sums(u)

    @pl.when(late)
    def _():
        for u in range(4):
            follow.send_direct(u)

    for u in range(4):
        follow.send_sums(u)

    def turn_copy(t, slot):
        return pltpu.make_async_remote_copy(
            src_ref=turned.at[t * rows:(t + 1) * rows], dst_ref=before.at[slot],
            send_sem=t_send.at[t], recv_sem=t_recv.at[slot],
            device_id=(nxt, t), device_id_type=MESH,
        )

    def mirror_copy(t, slot):
        return pltpu.make_async_remote_copy(
            src_ref=own_turned.at[t * rows:(t + 1) * rows], dst_ref=mirrored.at[slot],
            send_sem=m_send.at[t], recv_sem=m_recv.at[slot],
            device_id=(v, t), device_id_type=MESH,
        )

    for h in range(2):
        stat = follow.total(2 * h) / jnp.sqrt(follow.total(2 * h + 1) + 1e-05)
        out_ref[:, 2 * width + h * half:2 * width + (h + 1) * half] = stat
        turned[cols(h), :] = stat.T.astype(BF16)
        for t in range(h * pairs, (h + 1) * pairs):
            turn_copy(t, s).start()
    stat = own.total(0) / jnp.sqrt(own.total(1) + 1e-05)
    if fold:
        own_turned[...] = stat.T.astype(BF16)
        for t in range(n):
            @pl.when(owns(s, t))
            def _():
                mirror_copy(t, s).start()
    out_ref[:, width:2 * width] = stat
    for t in range(n):
        turn_copy(t, t).wait_recv()
        out_ref[:, t * rows:(t + 1) * rows] = before[t].astype(F32)
    if fold:
        for t in range(n):
            @pl.when(owns(t, s))
            def _():
                mirror_copy(t, t).wait_recv()
                out_ref[:, width + t * rows:width + (t + 1) * rows] = mirrored[t].astype(F32)

            @pl.when(owns(s, t))
            def _():
                mirror_copy(t, t).wait_send()

    for h in range(2):
        shift(h).wait_send()
    own.finish(2)
    follow.finish(4)
    for t in range(n):
        turn_copy(t, t).wait_send()


REDUCER = (0, 0, 0, 3, 1, 2, 3, 2, 3, 3, 0, 0, 2, 3, 0, 1, 1, 3, 0, 2, 2, 3, 3, 3, 3, 3)
PLAN = (
    (3, 6, 8, 9, 5, 7, 4, -1, 22, 13, 17, 21, 25, -2, 23, 24, 19, 12, 20, 15, 16, 0, 1, 2, 10, 14, 18, 11),
    (3, 6, 8, 9, 5, 7, 4, -1, 22, 13, 17, 21, 25, -2, 23, 24, 19, 12, 20, 15, 16, 0, 1, 2, 10, 14, 18, 11),
    (3, 6, 8, 9, 5, 7, -1, 22, 13, 0, 17, 21, 1, 25, 2, -2, 23, 4, 24, 10, 19, 14, 18, 12, 11, 20, 15, 16),
    (3, 6, 8, 9, 5, 7, 0, 1, 2, 4, -1, 22, 13, 17, 21, 25, -2, 23, 10, 24, 14, 19, 18, 12, 11, 20, 15, 16),
    (0, 1, 2, 3, 4, 6, 8, -1, 10, 9, 14, 5, 18, 7, -2, 11, 22, 15, 13, 16, 17, 21, 25, 23, 24, 19, 12, 20),
    (0, 1, 3, 2, 6, 4, 8, 9, 5, 7, -1, 10, 22, 14, 18, 13, 17, -2, 11, 21, 15, 16, 25, 23, 24, 19, 12, 20),
    (0, 1, 2, 4, 5, 7, -1, 10, 14, 18, -2, 11, 15, 16, 19, 12, 20, 3, 6, 8, 9, 22, 13, 17, 21, 25, 23, 24),
    (0, 1, 2, 4, 5, 7, -1, 10, 14, 18, -2, 11, 15, 16, 19, 12, 20, 3, 6, 8, 9, 22, 13, 17, 21, 25, 23, 24),
)


def line_kernel(
    nv, n, dosage_ref, class_hbm, effect_hbm, out_ref,
    d_ref, class_ref, effect_ref, after, wt, qt, sq, sq_after, dt, w_after, trait_column, parts,
    wire, near, joined, far, d_wire, d_near, d_joined, d_far, stat_out, stat_in,
    open_sem, load_sem, d_send, d_recv, near_send, near_recv, far_send, far_recv, stat_send, stat_recv,
):
    depth, width = d_ref.shape
    rows, half = width // n, width // 2
    v, s = lax.axis_index("var"), lax.axis_index("smp")
    nxt, prv = lax.rem(v + 1, nv), lax.rem(v + nv - 1, nv)

    loads = [
        pltpu.make_async_copy(dosage_ref, d_ref, load_sem.at[0]),
        pltpu.make_async_copy(class_hbm, class_ref, load_sem.at[1]),
        pltpu.make_async_copy(effect_hbm, effect_ref, load_sem.at[2]),
    ]
    for load in loads:
        load.start()
    barrier = pltpu.get_barrier_semaphore()
    host = n - 1

    def greet(target):
        pl.semaphore_signal(barrier, inc=1, device_id=target, device_id_type=MESH)

    greet((nxt, s))
    greet((prv, host))
    for role in range(n):
        @pl.when(s == role)
        def _():
            for other in {role - 1, role + 1, host} - {-1, n, role}:
                greet((v, other))

    for load in loads:
        load.wait()

    tiles = [(True, a, b) for a in range(n) for b in range(a, n)] + [(False, a, b) for a in range(n) for b in range(n)]
    order = {tile: at for at, tile in enumerate(tiles)}
    number = {tile: at for at, tile in enumerate(t for t in tiles if not diagonal(t))}
    spread = [b for h in range(n // 2) for b in (h, n - 1 - h)]

    def at_of(tile):
        return REDUCER[order[tile]]

    def block(index):
        return slice(index * rows, (index + 1) * rows)

    def cols(h):
        return slice(h * half, (h + 1) * half)

    def roles(body):
        for role in range(n):
            pl.when(s == role)(functools.partial(body, role))

    def plans(body):
        for at in range(2 * n):
            pl.when(2 * s + lax.rem(v, 2) == at)(functools.partial(body, at // 2, PLAN[at]))

    line = lax.broadcasted_iota(jnp.int32, (rows, rows), 0)
    column = lax.broadcasted_iota(jnp.int32, (rows, rows), 1)

    def slot(buffers, tile):
        plain, packed = buffers
        return packed.at[tile[1]] if diagonal(tile) else plain.at[number[tile]]

    def part(tile):
        same, a, b = tile
        first = 0 if same else 2
        b = b if same else spread.index(b)
        x, f = parts[first, block(a), block(b)], parts[first + 1, block(a), block(b)]
        if not diagonal(tile):
            return x, f
        middle = jnp.sum(jnp.where(line == column, f, 0.0), axis=0, keepdims=True)
        return jnp.where(line <= column, x, f), jnp.broadcast_to(middle, (EXTRA, rows))

    def places(tile):
        return (slice(0, rows), slice(rows, rows + EXTRA)) if diagonal(tile) else (0, 1)

    def put(buffers, tile, values):
        for where, value in zip(places(tile), values):
            slot(buffers, tile)[where] = value.astype(BF16)

    def get(buffers, tile):
        return [slot(buffers, tile)[where].astype(F32) for where in places(tile)]

    WIRE, NEAR, JOINED, FAR = (wire, d_wire), (near, d_near), (joined, d_joined), (far, d_far)

    def near_copy(tile, target):
        return pltpu.make_async_remote_copy(
            src_ref=slot(WIRE, tile), dst_ref=slot(NEAR, tile),
            send_sem=near_send.at[order[tile]], recv_sem=near_recv.at[order[tile]],
            device_id=(v, target), device_id_type=MESH,
        )

    def far_copy(tile, target):
        return pltpu.make_async_remote_copy(
            src_ref=slot(JOINED, tile), dst_ref=slot(FAR, tile),
            send_sem=far_send.at[order[tile]], recv_sem=far_recv.at[order[tile]],
            device_id=(v, target), device_id_type=MESH,
        )

    def stat_copy(tile, turned, target, to):
        return pltpu.make_async_remote_copy(
            src_ref=stat_out.at[order[tile], turned], dst_ref=stat_in.at[to],
            send_sem=stat_send.at[order[tile], turned], recv_sem=stat_recv.at[to],
            device_id=target, device_id_type=MESH,
        )

    def shift(at):
        return pltpu.make_async_remote_copy(
            src_ref=d_ref.at[:, block(spread[at])], dst_ref=after.at[:, block(at)],
            send_sem=d_send.at[at], recv_sem=d_recv.at[at],
            device_id=(prv, s), device_id_type=MESH,
        )

    def outer(role):
        return role in (0, n - 1)

    def kind(role, tile):
        target = at_of(tile)
        if target == role:
            return end
        if outer(role):
            return start
        return hand_on if target == role ^ 1 else join

    def mine(role, *acts):
        return [tile for tile in tiles if kind(role, tile) in acts]

    def start(role, tile):
        put(WIRE, tile, part(tile))
        near_copy(tile, role ^ 1).start()

    def join(role, tile):
        near_copy(tile, role ^ 1).wait_recv()
        put(JOINED, tile, [x + y for x, y in zip(part(tile), get(NEAR, tile))])
        far_copy(tile, n - 1 - role).start()

    def hand_on(role, tile):
        far_copy(tile, n - 1 - role).wait_recv()
        put(WIRE, tile, [x + y for x, y in zip(part(tile), get(FAR, tile))])
        near_copy(tile, role ^ 1).start()

    def goals(role, tile):
        same, a, b = tile
        if not same:
            return [(0, (v, a), a == role, 2 * n + b), (1, (nxt, b), False, a)]
        return [(0, (v, a), a == role, n + b)] + ([(1, (v, b), b == role, n + a)] if a != b else [])

    def end(role, tile):
        near_copy(tile, role ^ 1).wait_recv()
        x, f = [p + q for p, q in zip(part(tile), get(NEAR, tile))]
        if not outer(role):
            far_copy(tile, n - 1 - role).wait_recv()
            x, f = [p + q for p, q in zip((x, f), get(FAR, tile))]
        if diagonal(tile):
            packed, middle = x, f[:1]
            mirrored = packed.T
            x = jnp.where(line <= column, packed, mirrored)
            f = jnp.where(line == column, middle, jnp.where(line > column, packed, mirrored))
        stat = x / jnp.sqrt(f + 1e-05)
        for turned, target, local, to in goals(role, tile):
            value = stat.T if turned else stat
            if local:
                out_ref[:, block(to)] = value
            else:
                stat_out[order[tile], turned] = value.astype(BF16)
                stat_copy(tile, turned, target, to).start()

    classes = effect_ref.shape[0]
    mean = effect_ref[0]
    for c in range(1, classes):
        mean = mean + effect_ref[c]
    mean = mean / classes
    picked = class_ref[...]
    trait = jnp.zeros(picked.shape, F32)
    for c in range(classes):
        trait = jnp.where(picked == c, effect_ref[c] - mean, trait)
    for at in range(0, width, LANES):
        values = d_ref[:, at:at + LANES].astype(F32).T
        wt[at:at + LANES, :] = (values * trait).astype(BF16)
        qt[at:at + LANES, :] = (values * values).astype(BF16)
        dt[at:at + LANES, :] = values.astype(BF16)
    trait_column[...] = jnp.broadcast_to(trait, (LANES, depth)).T

    def squares(values):
        values = values.astype(F32)
        return (values * values).astype(BF16)

    sq[...] = squares(d_ref[...])
    for h in range(2):
        parts[0, cols(h), h * half:] = jnp.dot(wt[cols(h), :], d_ref[:, h * half:], preferred_element_type=F32)
        parts[1, cols(h), h * half:] = jnp.dot(qt[cols(h), :], sq[:, h * half:], preferred_element_type=F32)

    def enter(role):
        if role != host:
            pl.semaphore_wait(barrier, len({role - 1, role + 1} - {-1}) + 1)
        else:
            pl.semaphore_wait(barrier, 2 * n)
            for other in range(host):
                pl.semaphore_signal(open_sem, inc=1, device_id=(v, other), device_id_type=MESH)

    def run(stage, which=None):
        def body(role, plan):
            if which is not None and outer(role) != which:
                return
            marks = [-1] + [plan.index(-1 - h) for h in range(2)] + [len(plan)]
            first_end = [at for at in plan if at >= 0 and kind(role, tiles[at]) is end][0]
            for at in plan[marks[stage] + 1:marks[stage + 1]]:
                if at == first_end and role != host:
                    pl.semaphore_wait(open_sem, 1)
                kind(role, tiles[at])(role, tiles[at])

        plans(body)

    def follow(h):
        for at in range(h * n // 2, (h + 1) * n // 2):
            shift(at).wait_recv()
        sq_after[:, cols(h)] = squares(after[:, cols(h)])
        for at in range(h * half, (h + 1) * half, LANES):
            w_after[:, at:at + LANES] = (after[:, at:at + LANES].astype(F32) * trait_column[...]).astype(BF16)
        cross = jnp.dot(wt[...], after[:, cols(h)], preferred_element_type=F32)
        cross = cross + jnp.dot(dt[...], w_after[:, cols(h)], preferred_element_type=F32)
        parts[2, :, cols(h)] = 0.5 * cross
        parts[3, :, cols(h)] = jnp.dot(qt[...], sq_after[:, cols(h)], preferred_element_type=F32)

    roles(enter)
    run(0, True)
    for at in range(n):
        shift(at).start()
    run(0, False)
    follow(0)
    run(1)
    follow(1)
    run(2)

    def close(role):
        for tile in tiles:
            for turned, target, local, to in goals(at_of(tile), tile):
                here = tile[2] if turned else tile[1]
                if here == role and not local:
                    arrived = pltpu.make_async_remote_copy(
                        src_ref=stat_in.at[to], dst_ref=stat_in.at[to],
                        send_sem=stat_send.at[0, 0], recv_sem=stat_recv.at[to],
                        device_id=(v, role ^ 1), device_id_type=MESH,
                    )
                    arrived.wait_recv()
                    out_ref[:, block(to)] = stat_in[to].astype(F32)
        for tile in mine(role, start, hand_on):
            near_copy(tile, role ^ 1).wait_send()
        for tile in mine(role, join):
            far_copy(tile, n - 1 - role).wait_send()
        for tile in mine(role, end):
            for turned, target, local, to in goals(role, tile):
                if not local:
                    stat_copy(tile, turned, target, to).wait_send()

    roles(close)
    for at in range(n):
        shift(at).wait_send()


def diagonal(tile):
    return tile[0] and tile[1] == tile[2]


def solution(mesh):
    nv, n = mesh.shape["var"], mesh.shape["smp"]

    def shards(dosage, trait_class, class_effect):
        depth, width = dosage.shape
        rows, half, pairs = width // n, width // 2, n // 2
        dma, vmem = pltpu.SemaphoreType.DMA, pltpu.VMEM

        def call(body, scratch):
            return pl.pallas_call(
                functools.partial(body, nv, n),
                out_shape=jax.ShapeDtypeStruct((rows, 3 * width), F32),
                in_specs=[pl.BlockSpec(memory_space=pltpu.HBM)] * 3,
                out_specs=pl.BlockSpec(memory_space=vmem),
                scratch_shapes=[
                    vmem((depth, width), BF16),
                    vmem((1, depth), jnp.int32),
                    pltpu.SMEM(class_effect.shape, F32),
                    vmem((depth, width), BF16),
                    vmem((width, depth), BF16),
                    vmem((width, depth), BF16),
                    vmem((depth, width), BF16),
                    *scratch,
                ],
                compiler_params=pltpu.CompilerParams(
                    collective_id=0, has_side_effects=True, vmem_limit_bytes=32 * 1024 * 1024
                ),
            )(*(pltpu.with_memory_space_constraint(x, pltpu.HBM) for x in (dosage, trait_class.reshape(1, depth), class_effect)))

        if n == 4 and rows % LANES == 0:
            tiles = n * (n + 1) // 2 + n * n
            return call(line_kernel, [
                vmem((depth, width), BF16),
                vmem((width, depth), BF16),
                vmem((depth, width), BF16),
                vmem((depth, LANES), F32),
                vmem((4, width, width), F32),
                *[vmem((tiles - n, 2, rows, rows), BF16)] * 4,
                *[vmem((n, rows + EXTRA, rows), BF16)] * 4,
                vmem((tiles, 2, rows, rows), BF16),
                vmem((3 * n, rows, rows), BF16),
                pltpu.SemaphoreType.REGULAR,
                dma((3,)), dma((n,)), dma((n,)),
                *[dma((tiles,))] * 4,
                dma((tiles, 2)), dma((3 * n,)),
            ])

        def buffers(units, wide):
            return [
                vmem((units, width, wide), F32),
                vmem((units, width, wide), BF16),
                vmem((units, pairs, 2, rows, wide), BF16),
                vmem((units, pairs, 2, rows, wide), BF16),
                vmem((units, pairs, rows, wide), BF16),
                vmem((units, rows, wide), BF16),
            ]

        def semaphores(units):
            return [
                dma((units, pairs, 2)), dma((units, pairs, 2)), dma((units, pairs, 2)),
                dma((units, pairs)), dma((units,)), dma((units,)),
            ]

        return call(kernel, [
            vmem((width, rows), BF16),
            vmem((n, rows, rows), BF16),
            vmem((width, rows), BF16),
            vmem((n, rows, rows), BF16),
            *buffers(2, width),
            *buffers(4, half),
            dma((3,)), dma((2,)), dma((2,)),
            dma((n,)), dma((n,)), dma((n,)), dma((n,)),
            *semaphores(2),
            *semaphores(4),
        ])

    in_specs = (P("smp", "var"), P("smp"), P())
    out_specs = P(("var", "smp"), None)
    return jax.shard_map(shards, mesh=mesh, in_specs=in_specs, out_specs=out_specs, check_vma=False)
```
